256 devices in a mesh: heads: 8 (over y, x_hi), inner: 4 (over x_lo, core), outer: 8 (over z).
Axes of the slice: x: 4 (x_hi: 2, x_lo: 2; x = x_hi * 2 + x_lo), y: 4, z: 8, core: 2. Of those that a mesh axis runs over, the one named last changes fastest.
Arguments:
- queries: bfloat16 [8192, 16384], P(('inner', 'outer'), 'heads'), may hold values from -6 to 6
- keys: bfloat16 [8192, 1024], P(('inner', 'outer'), 'heads'), may hold values from -6 to 6
- values: bfloat16 [8192, 1024], P(('inner', 'outer'), 'heads'), may hold values from -6 to 6
- block_chain: int32 [64], replicated, may hold values from 0 to 8, as said below
- block_depth: int32 [64], replicated, may hold values from 0 to 35
Outputs:
- attended: bfloat16 [8192, 16384], P(('inner', 'outer'), 'heads')
The draws below stay inside these ranges and needn't reach their ends.
Inputs may be any that keep to these rules, and one draw needn't show every extreme that they name: block_chain and block_depth together describe the tree: 32 prefix blocks with chain 0 and depths 0 to 31, and for each chain c of 1 to 8 its 4 blocks with depths 32 to 35; each pair of chain and depth names one stored block, in any order of storage.
All inputs are finite; a program needn't handle non-finite values.
Results may differ from the reference program's by a relative error of at most 0.0065.
Values may be sent and summed in bfloat16 or wider, within the bound.
No kernel may reach another device: no remote copies, remote signals or barrier semaphores. Data moves between devices by JAX's collectives and lax.ppermute only.
A program may use at most 64 MiB of HBM per device.

```python
import jax
import jax.numpy as jnp
from jax import lax

HD = 128
QH = 16
BLOCK = 128
CHAIN_BLOCKS = 4
KV_HEADS = 8
QHEADS = 128
NB = 64
PREFIX_BLOCKS = 32
TOKENS = 8192


def tree_layout(key):
    canonical = jnp.arange(NB, dtype=jnp.int32)
    chain_ids = jnp.where(canonical < PREFIX_BLOCKS, 0, 1 + (canonical - PREFIX_BLOCKS) // CHAIN_BLOCKS)
    depth_ids = jnp.where(canonical < PREFIX_BLOCKS, canonical, PREFIX_BLOCKS + (canonical - PREFIX_BLOCKS) % CHAIN_BLOCKS)
    ordering = jax.random.permutation(jax.random.fold_in(key, 7), NB)
    return (chain_ids[ordering].astype(jnp.int32), depth_ids[ordering].astype(jnp.int32))


def draw_block_chain(key, part):
    return tree_layout(key)[0]


def draw_block_depth(key, part):
    return tree_layout(key)[1]


def rough_entries(key, columns):
    return jnp.clip(jax.random.normal(jax.random.fold_in(key, 3), (TOKENS, columns), jnp.float32), -6.0, 6.0)


def draw_queries(key, part):
    entries = rough_entries(jax.random.fold_in(key, 21), QHEADS * HD)
    return entries.astype(jnp.bfloat16)


def draw_keys(key, part):
    entries = rough_entries(jax.random.fold_in(key, 22), KV_HEADS * HD)
    return entries.astype(jnp.bfloat16)


def shard_levels(key, shape, cuts, smallest, high):
    def one(dim, parts):
        draws = jax.random.uniform(jax.random.fold_in(jax.random.fold_in(key, 6), dim), (parts,), jnp.float32, smallest / len(cuts), high / len(cuts))
        return jnp.repeat(jnp.exp(draws), shape[dim] // parts).reshape((-1,) + (1,) * (len(shape) - dim - 1))

    gain = one(*cuts[0])
    for cut in cuts[1:]:
        gain = gain * one(*cut)
    return gain


def normal_values(stream_key, shape, spread, bound, pieces=(), kind=jnp.bfloat16):
    values = spread * jax.random.normal(stream_key, shape, jnp.float32)
    if pieces:
        values = values * shard_levels(stream_key, shape, pieces, -0.22, 0.18)
    return jnp.clip(values, -bound, bound).astype(kind)


def setup_inputs(seed: int = 0) -> dict:
    streams_of = jax.random.split(jax.random.key(seed), 6)
    queries = draw_queries(jax.random.fold_in(streams_of[5], 71), 0)
    keys = draw_keys(jax.random.fold_in(streams_of[5], 71), 0)
    values = normal_values(streams_of[2], (TOKENS, KV_HEADS * HD), 1.0, 6.0, ((0, 32), (1, 8)))
    block_chain = draw_block_chain(jax.random.fold_in(streams_of[5], 71), 0)
    block_depth = draw_block_depth(jax.random.fold_in(streams_of[5], 71), 0)
    return dict(queries=queries, keys=keys, values=values, block_chain=block_chain, block_depth=block_depth)


def reference(queries, keys, values, block_chain, block_depth):
    scaling = HD ** -0.5
    token_pos = jnp.arange(BLOCK, dtype=jnp.int32)
    most_blocks = PREFIX_BLOCKS + CHAIN_BLOCKS
    results = []
    for head_group in range(KV_HEADS):
        key_blocks = keys[:, head_group * HD:(head_group + 1) * HD].astype(jnp.float32).reshape(NB, BLOCK, HD)
        value_blocks = values[:, head_group * HD:(head_group + 1) * HD].astype(jnp.float32).reshape(NB, BLOCK, HD)
        query_group = queries[:, head_group * QH * HD:(head_group + 1) * QH * HD].reshape(NB, BLOCK, QH, HD)

        def one_block(inputs):
            query_block, block_id = inputs
            same_tree = (block_chain == 0) | (block_chain == block_chain[block_id])
            block_seen = same_tree & (block_depth <= block_depth[block_id])
            ranking = jnp.where(block_seen, 0, NB) + jnp.arange(NB, dtype=jnp.int32)
            picked = jnp.argsort(ranking)[:most_blocks].astype(jnp.int32)
            key_sel = key_blocks[picked].reshape(most_blocks * BLOCK, HD)
            value_sel = value_blocks[picked].reshape(most_blocks * BLOCK, HD)
            picked_seen = block_seen[picked]
            is_self = picked == block_id
            visible = picked_seen[None, :, None] & ((~is_self)[None, :, None] | (token_pos[None, None, :] <= token_pos[:, None, None]))
            visible = visible.reshape(BLOCK, most_blocks * BLOCK)
            scores = jnp.einsum("qhd,kd->hqk", query_block.astype(jnp.float32), key_sel) * scaling
            scores = jnp.where(visible[None], scores, -jnp.inf)
            row_max = jnp.max(scores, axis=2, keepdims=True)
            expon = jnp.exp(scores - row_max)
            row_total = jnp.sum(expon, axis=2)
            rounded = lax.optimization_barrier(expon.astype(jnp.bfloat16))
            weights = rounded.astype(jnp.float32)
            mixed = jnp.einsum("hqk,kd->qhd", weights, value_sel) / jnp.transpose(row_total)[:, :, None]
            return mixed.astype(jnp.bfloat16)

        out_group = lax.map(one_block, (query_group, jnp.arange(NB, dtype=jnp.int32)))
        results.append(out_group.reshape(TOKENS, QH * HD))
    return jnp.concatenate(results, axis=1)
```

```python
import functools
import math

import jax
import jax.numpy as jnp
from jax import lax
from jax.experimental import pallas as pl
from jax.experimental.pallas import tpu as pltpu
from jax.sharding import PartitionSpec as P

BLOCK = 128
HEAD = 128
TILE = 8
LOWEST = -1e30
AXES = ("inner", "outer")
OFFSETS = (0, -1, 1, -2, 2, -3, 3, 4)


def dot(a, b, contract):
    return lax.dot_general(a, b, (contract, ((), ())), preferred_element_type=jnp.float32)


def attend_kernel(chain_ref, depth_ref, q_ref, *rest, pieces, heads, count_in):
    piece_refs = rest[:count_in]
    o_ref, kv_buf, order, row_max, acc, sem = rest[count_in:]
    copies = []
    start = 0
    for ref in piece_refs:
        rows = ref.shape[0]
        copies.append(pltpu.make_async_copy(ref, kv_buf.at[pl.ds(start, rows), :], sem))
        copies[-1].start()
        start += rows
    inner = lax.axis_index("inner")
    outer = lax.axis_index("outer")
    counts = []
    q_chain, q_depth = [], []
    for qb in range(2):
        own = (inner * 8 + outer) * 2 + qb
        q_chain.append(chain_ref[own])
        q_depth.append(depth_ref[own])
        counts.append(jnp.int32(0))
    slot = 0
    for flip, offset, blocks in pieces:
        source = (jnp.bitwise_xor(inner, flip) * 8 + lax.rem(outer + offset + 8, 8)) * 2
        for b in blocks:
            chain = chain_ref[source + b]
            depth = depth_ref[source + b]
            for qb in range(2):
                seen = ((chain == 0) | (chain == q_chain[qb])) & (depth < q_depth[qb])
                order[qb, counts[qb]] = slot
                counts[qb] = counts[qb] + seen.astype(jnp.int32)
            slot += 1
    for copy in copies:
        copy.wait()
    scale = HEAD ** -0.5 * math.log2(math.e)
    ones = jnp.ones((TILE * BLOCK, HEAD), jnp.bfloat16)

    def tile(qb, slots, limit):
        rows = pl.ds(pl.multiple_of(qb * BLOCK, BLOCK), BLOCK)
        kv = [kv_buf[pl.ds(pl.multiple_of(s * BLOCK, BLOCK), BLOCK), :] for s in slots]
        k = jnp.concatenate([x[:, :HEAD] for x in kv], axis=0)
        v = jnp.concatenate([x[:, HEAD:] for x in kv], axis=0)
        v = jnp.concatenate([v, ones], axis=1)
        if limit is not None:
            col = lax.broadcasted_iota(jnp.int32, (BLOCK, TILE * BLOCK), 1)
            row = lax.broadcasted_iota(jnp.int32, (BLOCK, TILE * BLOCK), 0)
            allowed = (col <= row) | ((col >= BLOCK) & (col < limit))
        for h in range(heads):
            s = dot(q_ref[rows, h * HEAD:(h + 1) * HEAD], k, ((1,), (1,)))
            if limit is not None:
                s = jnp.where(allowed, s, LOWEST)
            before = row_max[h]
            after = jnp.maximum(before, jnp.max(s, axis=1, keepdims=True))
            weights = jnp.exp2((s - after[:, :1]) * scale).astype(jnp.bfloat16)
            rescale = jnp.exp2((before - after) * scale)
            row_max[h] = after
            part = dot(weights, v, ((1,), (0,)))
            acc[h, :, :HEAD] = acc[h, :, :HEAD] * rescale + part[:, :HEAD]
            acc[h, :, HEAD:] = acc[h, :, HEAD:] * rescale + part[:, HEAD:]

    def one_block(qb, _):
        row_max[...] = jnp.full(row_max.shape, LOWEST, jnp.float32)
        acc[...] = jnp.zeros(acc.shape, jnp.float32)
        count = jnp.where(qb == 0, counts[0], counts[1])
        full = lax.div(count, TILE)
        left = count - full * TILE

        def step(t, _):
            tile(qb, [order[qb, t * TILE + i] for i in range(TILE)], None)
            return 0

        lax.fori_loop(0, full, step, 0)
        last = [qb] + [
            jnp.where(i < left, order[qb, full * TILE + i], qb) for i in range(TILE - 1)
        ]
        tile(qb, last, (left + 1) * BLOCK)
        rows = pl.ds(pl.multiple_of(qb * BLOCK, BLOCK), BLOCK)
        for h in range(heads):
            o_ref[rows, h * HEAD:(h + 1) * HEAD] = (
                acc[h, :, :HEAD] / acc[h, :, HEAD:]
            ).astype(jnp.bfloat16)
        return 0

    lax.fori_loop(0, 2, one_block, 0)


def attend(queries, chain, depth, pieces, arrays):
    rows, width = queries.shape
    heads = width // HEAD
    vmem = pl.BlockSpec(memory_space=pltpu.VMEM)
    smem = pl.BlockSpec(memory_space=pltpu.SMEM)
    anywhere = pl.BlockSpec(memory_space=pl.ANY)
    keys = sum(a.shape[0] for a in arrays)
    return pl.pallas_call(
        functools.partial(attend_kernel, pieces=pieces, heads=heads, count_in=len(arrays)),
        out_shape=jax.ShapeDtypeStruct((rows, width), jnp.bfloat16),
        in_specs=[smem, smem, vmem] + [anywhere] * len(arrays),
        out_specs=vmem,
        scratch_shapes=[
            pltpu.VMEM((keys, 2 * HEAD), jnp.bfloat16),
            pltpu.SMEM((2, 80), jnp.int32),
            pltpu.VMEM((heads, BLOCK, HEAD), jnp.float32),
            pltpu.VMEM((heads, BLOCK, 2 * HEAD), jnp.float32),
            pltpu.SemaphoreType.DMA(()),
        ],
        compiler_params=pltpu.CompilerParams(vmem_limit_bytes=48 << 20),
        name="tree_attention",
    )(chain, depth, queries, *arrays)


def send(x, route):
    pairs = []
    for i in range(4):
        for o in range(8):
            j, p = route(i, o)
            pairs.append((i * 8 + o, j * 8 + p % 8))
    return lax.ppermute(x, AXES, pairs)


def to_core(x):
    return send(x, lambda i, o: (i ^ 1, o))


def to_x(x):
    return send(x, lambda i, o: (i ^ 2, o))


def up(x):
    return send(x, lambda i, o: (i, o + 1))


def down(x):
    return send(x, lambda i, o: (i, o - 1))


def local(queries, keys, values, block_chain, block_depth):
    kv = jnp.concatenate([keys, values], axis=1)
    half = kv.shape[0]
    pair = jnp.concatenate([kv, to_x(kv)], axis=0)
    found = [(0, pair)]
    rising = falling = pair
    for d in (1, 2, 3):
        rising, falling = up(rising), down(falling)
        found += [(-d, rising), (d, falling)]
    far = (up(rising[:half]), down(falling[half:]))
    arrays, pieces = [], []
    for offset, x in found:
        for core in (0, 1):
            arrays.append(to_core(x) if core else x)
            pieces += [(core, offset, (0, 1)), (2 ^ core, offset, (0, 1))]
    for flip, x in zip((0, 2), far):
        for core in (0, 1):
            arrays.append(to_core(x) if core else x)
            pieces.append((flip ^ core, 4, (0, 1)))
    return attend(queries, block_chain, block_depth, tuple(pieces), arrays)


def solution(mesh):
    return jax.shard_map(
        local,
        mesh=mesh,
        in_specs=(
            P(("inner", "outer"), "heads"),
            P(("inner", "outer"), "heads"),
            P(("inner", "outer"), "heads"),
            P(),
            P(),
        ),
        out_specs=P(("inner", "outer"), "heads"),
        check_vma=False,
    )
```

```python
import functools
import math

import jax
import jax.numpy as jnp
from jax import lax
from jax.experimental import pallas as pl
from jax.experimental.pallas import tpu as pltpu
from jax.sharding import PartitionSpec as P

BLOCK = 128
HEAD = 128
TILE = 8
LOWEST = -1e30
AXES = ("inner", "outer")


def dot(a, b, contract):
    return lax.dot_general(a, b, (contract, ((), ())), preferred_element_type=jnp.float32)


def plan_order(chain_ref, depth_ref, order, stages):
    inner = lax.axis_index("inner")
    outer = lax.axis_index("outer")
    q_chain, q_depth, counts = [], [], []
    for qb in range(2):
        own = (inner * 8 + outer) * 2 + qb
        q_chain.append(chain_ref[own])
        q_depth.append(depth_ref[own])
        counts.append(jnp.int32(0))
    slot = 0
    for j, pieces in enumerate(stages):
        for flip, offset in pieces:
            source = (jnp.bitwise_xor(inner, flip) * 8 + lax.rem(outer + offset + 8, 8)) * 2
            for b in range(2):
                chain = chain_ref[source + b]
                depth = depth_ref[source + b]
                for qb in range(2):
                    seen = ((chain == 0) | (chain == q_chain[qb])) & (depth < q_depth[qb])
                    order[qb, counts[qb]] = slot
                    counts[qb] = counts[qb] + seen.astype(jnp.int32)
                slot += 1
        for qb in range(2):
            order[qb, 64 + j] = counts[qb]


def attend_kernel(*refs, stage, stages, start, count_in, heads):
    first, final = stage == 0, stage == len(stages) - 1
    refs = list(refs)
    if first:
        chain_ref, depth_ref = refs[:2]
        refs = refs[2:]
    else:
        order = refs.pop(0)
        refs = refs[: 1 + count_in] + refs[4 + count_in:]
    q_ref = refs[0]
    piece_refs = refs[1: 1 + count_in]
    refs = refs[1 + count_in:]
    if final:
        o_ref = refs.pop(0)
    kv_buf, row_max, acc = refs[:3]
    refs = refs[3:]
    if first:
        order = refs.pop(0)
    sem = refs.pop(0)
    copies = []
    for ref in piece_refs:
        rows = ref.shape[0]
        copies.append(pltpu.make_async_copy(ref, kv_buf.at[pl.ds(start, rows), :], sem))
        copies[-1].start()
        start += rows
    if first:
        plan_order(chain_ref, depth_ref, order, stages)
        row_max[...] = jnp.full(row_max.shape, LOWEST, jnp.float32)
        acc[...] = jnp.zeros(acc.shape, jnp.float32)
    for copy in copies:
        copy.wait()
    scale = HEAD ** -0.5 * math.log2(math.e)
    ones = jnp.ones((TILE * BLOCK, HEAD), jnp.bfloat16)

    def tile(qb, slots, limit, triangle):
        rows = pl.ds(pl.multiple_of(qb * BLOCK, BLOCK), BLOCK)
        kv = [kv_buf[pl.ds(pl.multiple_of(s * BLOCK, BLOCK), BLOCK), :] for s in slots]
        k = jnp.concatenate([x[:, :HEAD] for x in kv], axis=0)
        v = jnp.concatenate([x[:, HEAD:] for x in kv], axis=0)
        v = jnp.concatenate([v, ones], axis=1)
        if limit is not None:
            col = lax.broadcasted_iota(jnp.int32, (BLOCK, TILE * BLOCK), 1)
            allowed = col < limit
            if triangle:
                row = lax.broadcasted_iota(jnp.int32, (BLOCK, TILE * BLOCK), 0)
                allowed = allowed & ((col >= BLOCK) | (col <= row))
        for h in range(heads):
            at = qb * heads + h
            s = dot(q_ref[rows, h * HEAD:(h + 1) * HEAD], k, ((1,), (1,)))
            if limit is not None:
                s = jnp.where(allowed, s, LOWEST)
            before = row_max[at]
            after = jnp.maximum(before, jnp.max(s, axis=1, keepdims=True))
            weights = jnp.exp2((s - after[:, :1]) * scale).astype(jnp.bfloat16)
            rescale = jnp.exp2((before - after) * scale)
            row_max[at] = after
            part = dot(weights, v, ((1,), (0,)))
            acc[at, :, :HEAD] = acc[at, :, :HEAD] * rescale + part[:, :HEAD]
            acc[at, :, HEAD:] = acc[at, :, HEAD:] * rescale + part[:, HEAD:]

    def one_block(qb, _):
        base = order[qb, 64]
        if first:
            slots = [qb] + [jnp.where(i < base, order[qb, i], qb) for i in range(TILE - 1)]
            tile(qb, slots, (base + 1) * BLOCK, True)
            return 0
        before = order[qb, 64 + stage - 1] - base
        now = order[qb, 64 + stage] - base
        full = lax.div(now, TILE)

        def step(t, _):
            tile(qb, [order[qb, base + t * TILE + i] for i in range(TILE)], None, False)
            return 0

        lax.fori_loop(lax.div(before, TILE), full, step, 0)
        if final:
            left = now - full * TILE

            @pl.when(left > 0)
            def _():
                at = base + full * TILE
                slots = [jnp.where(i < left, order[qb, at + i], qb) for i in range(TILE)]
                tile(qb, slots, left * BLOCK, False)

            rows = pl.ds(pl.multiple_of(qb * BLOCK, BLOCK), BLOCK)
            for h in range(heads):
                at = qb * heads + h
                o_ref[rows, h * HEAD:(h + 1) * HEAD] = (
                    acc[at, :, :HEAD] / acc[at, :, HEAD:]
                ).astype(jnp.bfloat16)
        return 0

    lax.fori_loop(0, 2, one_block, 0)


def attend(queries, chain, depth, stages, stage, arrays, state):
    rows, width = queries.shape
    heads = width // HEAD
    first, final = stage == 0, stage == len(stages) - 1
    vmem = pl.BlockSpec(memory_space=pltpu.VMEM)
    smem = pl.BlockSpec(memory_space=pltpu.SMEM)
    anywhere = pl.BlockSpec(memory_space=pl.ANY)
    slots = 2 * sum(len(p) for p in stages)
    start = 2 * BLOCK * sum(len(p) for p in stages[:stage])
    held = [
        pltpu.VMEM((slots * BLOCK, 2 * HEAD), jnp.bfloat16),
        pltpu.VMEM((2 * heads, BLOCK, HEAD), jnp.float32),
        pltpu.VMEM((2 * heads, BLOCK, 2 * HEAD), jnp.float32),
    ]
    out = jax.ShapeDtypeStruct((rows, width), jnp.bfloat16)
    n = len(arrays)
    body = functools.partial(
        attend_kernel, stage=stage, stages=stages, start=start, count_in=n, heads=heads
    )
    params = pltpu.CompilerParams(vmem_limit_bytes=16 << 20)
    sem = pltpu.SemaphoreType.DMA(())
    pairs = len(stages[stage]) * 2
    cost = pl.CostEstimate(
        flops=pairs * 4 * heads * BLOCK * BLOCK * HEAD,
        transcendentals=pairs * heads * BLOCK * BLOCK,
        bytes_accessed=pairs * BLOCK * HEAD * 4 + rows * width * 2,
    )
    if first:
        return pl.pallas_call(
            body,
            out_shape=held + [jax.ShapeDtypeStruct((2, 128), jnp.int32)],
            in_specs=[smem, smem, vmem] + [anywhere] * n,
            out_specs=[vmem] * 3 + [smem],
            scratch_shapes=[sem],
            compiler_params=params,
            cost_estimate=cost,
            name="attend_first",
        )(chain, depth, queries, *arrays)
    kv_buf, row_max, acc, order = state
    result = pl.pallas_call(
        body,
        out_shape=([out] if final else []) + held,
        in_specs=[smem, vmem] + [anywhere] * n + [vmem] * 3,
        out_specs=[vmem] * (4 if final else 3),
        input_output_aliases={2 + n + i: i + final for i in range(3)},
        scratch_shapes=[sem],
        compiler_params=params,
        cost_estimate=cost,
        name="attend_last" if final else "attend_next",
    )(order, queries, *arrays, kv_buf, row_max, acc)
    return result[0] if final else (*result, order)


def send(x, route):
    pairs = []
    for i in range(4):
        for o in range(8):
            j, p = route(i, o)
            pairs.append((i * 8 + o, j * 8 + p % 8))
    return lax.ppermute(x, AXES, pairs)


def to_core(x):
    return send(x, lambda i, o: (i ^ 1, o))


def to_x(x):
    return send(x, lambda i, o: (i ^ 2, o))


def up(x):
    return send(x, lambda i, o: (i, o + 1))


def down(x):
    return send(x, lambda i, o: (i, o - 1))


def local(queries, keys, values, block_chain, block_depth):
    kv = jnp.concatenate([keys, values], axis=1)
    half = kv.shape[0]
    pair = jnp.concatenate([kv, to_x(kv)], axis=0)
    stages = [[(0, 0), (2, 0), (1, 0), (3, 0)]]
    for d in (1, 2, 3):
        stages.append([(f, sign * d) for sign in (-1, 1) for f in (0, 2, 1, 3)])
    stages.append([(f, 4) for f in (0, 1, 2, 3)])
    run = functools.partial(attend, queries, block_chain, block_depth, stages)
    rising = falling = pair
    arrays, state = [pair, to_core(pair)], None
    for d in range(4):
        if d < 3:
            rising, falling = up(rising), down(falling)
        else:
            rising, falling = up(rising[:half]), down(falling[half:])
        state = run(d, arrays, state)
        rising, falling, state = lax.optimization_barrier((rising, falling, state))
        arrays = [rising, to_core(rising), falling, to_core(falling)]
    return run(4, arrays, state)


def solution(mesh):
    return jax.shard_map(
        local,
        mesh=mesh,
        in_specs=(
            P(("inner", "outer"), "heads"),
            P(("inner", "outer"), "heads"),
            P(("inner", "outer"), "heads"),
            P(),
            P(),
        ),
        out_specs=P(("inner", "outer"), "heads"),
        check_vma=False,
    )
```

```python
import functools
import math

import jax
import jax.numpy as jnp
from jax import lax
from jax.experimental import pallas as pl
from jax.experimental.pallas import tpu as pltpu
from jax.sharding import PartitionSpec as P

BLOCK = 128
HEAD = 128
TILE = 4
UNIT = 4 * BLOCK
LOWEST = -1e30
AXES = ("inner", "outer")


def dot(a, b, contract):
    return lax.dot_general(a, b, (contract, ((), ())), preferred_element_type=jnp.float32)


def plan_order(chain_ref, depth_ref, order, stages):
    inner = lax.axis_index("inner")
    outer = lax.axis_index("outer")
    q_chain, q_depth, counts = [], [], []
    for qb in range(2):
        own = (inner * 8 + outer) * 2 + qb
        q_chain.append(chain_ref[own])
        q_depth.append(depth_ref[own])
        counts.append(jnp.int32(0))
    row = 0
    for j, pieces in enumerate(stages):
        for flip, offset in pieces:
            source = (jnp.bitwise_xor(inner, flip) * 8 + lax.rem(outer + offset + 8, 8)) * 2
            for b in range(2):
                chain = chain_ref[source + b]
                depth = depth_ref[source + b]
                for qb in range(2):
                    seen = ((chain == 0) | (chain == q_chain[qb])) & (depth < q_depth[qb])
                    order[qb, counts[qb]] = row + b * BLOCK
                    counts[qb] = counts[qb] + seen.astype(jnp.int32)
            row += UNIT
        for qb in range(2):
            order[qb, 64 + j] = counts[qb]


def attend_kernel(*refs, stage, stages, start, count_in, heads):
    first, final = stage == 0, stage == len(stages) - 1
    refs = list(refs)
    if first:
        chain_ref, depth_ref = refs[:2]
        refs = refs[2:]
    else:
        order = refs.pop(0)
        refs = refs[: 1 + count_in] + refs[4 + count_in:]
    q_ref = refs[0]
    piece_refs = refs[1: 1 + count_in]
    refs = refs[1 + count_in:]
    if final:
        o_ref = refs.pop(0)
    kv_buf, shift, acc = refs[:3]
    refs = refs[3:]
    if first:
        order = refs.pop(0)
    sem = refs.pop(0)
    copies = []
    for ref in piece_refs:
        rows = ref.shape[0]
        copies.append(pltpu.make_async_copy(ref, kv_buf.at[pl.ds(start, rows), :], sem))
        copies[-1].start()
        start += rows
    if first:
        plan_order(chain_ref, depth_ref, order, stages)
    for copy in copies:
        copy.wait()
    scale = HEAD ** -0.5 * math.log2(math.e)
    width = heads * BLOCK

    def heads_of(qb):
        rows = pl.ds(pl.multiple_of(qb * BLOCK, BLOCK), BLOCK)
        return jnp.concatenate([q_ref[rows, h * HEAD:(h + 1) * HEAD] for h in range(heads)], axis=0)

    def keys_of(row):
        return kv_buf[pl.ds(pl.multiple_of(row, BLOCK), BLOCK), :]

    def values_of(row):
        return kv_buf[pl.ds(pl.multiple_of(row + 2 * BLOCK, BLOCK), BLOCK), :]

    def with_ones(v):
        return jnp.concatenate([v, jnp.ones((16, v.shape[1]), v.dtype)], axis=0)

    def diagonal(qb):
        row = qb * BLOCK
        s = dot(keys_of(row), heads_of(qb), ((1,), (1,)))
        key = lax.broadcasted_iota(jnp.int32, s.shape, 0)
        query = lax.broadcasted_iota(jnp.int32, s.shape, 1)
        s = jnp.where(key <= lax.rem(query, BLOCK), s, LOWEST)
        top = jnp.max(s, axis=0, keepdims=True)
        weights = jnp.exp2((s - top) * scale).astype(jnp.bfloat16)
        shift[qb] = top
        acc[qb] = dot(with_ones(values_of(row)), weights, ((1,), (0,)))

    def tile_of(qb, at, left):
        rows = [order[qb, at]]
        rows += [jnp.where(i < left, order[qb, at + i], rows[0]) for i in range(1, TILE)]
        k = jnp.concatenate([keys_of(r) for r in rows], axis=0)
        v = with_ones(jnp.concatenate([values_of(r) for r in rows], axis=1))
        col = lax.broadcasted_iota(jnp.int32, v.shape, 1)
        v = jnp.where(col < left * BLOCK, v, jnp.zeros_like(v))
        return k, v

    def fast_tile(qb, at, left):
        k, v = tile_of(qb, at, left)
        s = dot(k, heads_of(qb), ((1,), (1,)))
        weights = jnp.exp2((s - shift[qb]) * scale).astype(jnp.bfloat16)
        acc[qb] += dot(v, weights, ((1,), (0,)))

    def safe_tile(qb, at, left):
        k, v = tile_of(qb, at, left)
        s = dot(k, heads_of(qb), ((1,), (1,)))
        before = shift[qb]
        after = jnp.maximum(before, jnp.max(s, axis=0, keepdims=True))
        weights = jnp.exp2((s - after) * scale).astype(jnp.bfloat16)
        shift[qb] = after
        acc[qb] = acc[qb] * jnp.exp2((before - after) * scale) + dot(v, weights, ((1,), (0,)))

    def one_block(qb, _):
        if first:
            diagonal(qb)
            done = 0
        else:
            done = lax.div(order[qb, 64 + stage - 1], TILE)
        now = order[qb, 64 + stage]
        until = lax.div(now + TILE - 1, TILE) if final else lax.div(now, TILE)

        def step(t, _):
            fast_tile(qb, t * TILE, now - t * TILE)
            return 0

        lax.fori_loop(done, until, step, 0)
        if final:
            total = acc[qb, HEAD:HEAD + 1, :]
            fine = jnp.min(jnp.where(total < 2.0 ** 64, 1.0, 0.0))

            @pl.when(fine < 0.5)
            def _():
                diagonal(qb)

                def again(t, _):
                    safe_tile(qb, t * TILE, now - t * TILE)
                    return 0

                lax.fori_loop(0, until, again, 0)

            mixed = acc[qb, :HEAD, :] / acc[qb, HEAD:HEAD + 1, :]
            rows = pl.ds(pl.multiple_of(qb * BLOCK, BLOCK), BLOCK)
            for h in range(heads):
                part = mixed[:, h * BLOCK:(h + 1) * BLOCK]
                o_ref[rows, h * HEAD:(h + 1) * HEAD] = part.T.astype(jnp.bfloat16)
        return 0

    lax.fori_loop(0, 2, one_block, 0)


def attend(queries, chain, depth, stages, stage, arrays, state):
    rows, width = queries.shape
    heads = width // HEAD
    first, final = stage == 0, stage == len(stages) - 1
    vmem = pl.BlockSpec(memory_space=pltpu.VMEM)
    smem = pl.BlockSpec(memory_space=pltpu.SMEM)
    anywhere = pl.BlockSpec(memory_space=pl.ANY)
    units = sum(len(p) for p in stages)
    start = UNIT * sum(len(p) for p in stages[:stage])
    held = [
        pltpu.VMEM((units * UNIT, HEAD), jnp.bfloat16),
        pltpu.VMEM((2, 1, heads * BLOCK), jnp.float32),
        pltpu.VMEM((2, HEAD + 16, heads * BLOCK), jnp.float32),
    ]
    out = jax.ShapeDtypeStruct((rows, width), jnp.bfloat16)
    n = len(arrays)
    body = functools.partial(
        attend_kernel, stage=stage, stages=stages, start=start, count_in=n, heads=heads
    )
    params = pltpu.CompilerParams(vmem_limit_bytes=32 << 20)
    sem = pltpu.SemaphoreType.DMA(())
    pairs = len(stages[stage]) * 2
    cost = pl.CostEstimate(
        flops=pairs * 4 * heads * BLOCK * BLOCK * HEAD,
        transcendentals=pairs * heads * BLOCK * BLOCK,
        bytes_accessed=pairs * BLOCK * HEAD * 4 + rows * width * 2,
    )
    if first:
        return pl.pallas_call(
            body,
            out_shape=held + [jax.ShapeDtypeStruct((2, 128), jnp.int32)],
            in_specs=[smem, smem, vmem] + [anywhere] * n,
            out_specs=[vmem] * 3 + [smem],
            scratch_shapes=[sem],
            compiler_params=params,
            cost_estimate=cost,
            name="attend_first",
        )(chain, depth, queries, *arrays)
    kv_buf, shift, acc, order = state
    result = pl.pallas_call(
        body,
        out_shape=([out] if final else []) + held,
        in_specs=[smem, vmem] + [anywhere] * n + [vmem] * 3,
        out_specs=[vmem] * (4 if final else 3),
        input_output_aliases={2 + n + i: i + final for i in range(3)},
        scratch_shapes=[sem],
        compiler_params=params,
        cost_estimate=cost,
        name="attend_last" if final else "attend_next",
    )(order, queries, *arrays, kv_buf, shift, acc)
    return result[0] if final else (*result, order)


def pack_kernel(k_ref, v_ref, o_ref):
    for b in range(2):
        rows = slice(b * BLOCK, (b + 1) * BLOCK)
        o_ref[b * BLOCK:(b + 1) * BLOCK, :] = k_ref[rows, :]
        o_ref[(2 + b) * BLOCK:(3 + b) * BLOCK, :] = v_ref[rows, :].T


def pack(keys, values):
    vmem = pl.BlockSpec(memory_space=pltpu.VMEM)
    return pl.pallas_call(
        pack_kernel,
        out_shape=jax.ShapeDtypeStruct((UNIT, HEAD), keys.dtype),
        in_specs=[vmem, vmem],
        out_specs=vmem,
        name="pack",
    )(keys, values)


def send(x, route):
    pairs = []
    for i in range(4):
        for o in range(8):
            j, p = route(i, o)
            pairs.append((i * 8 + o, j * 8 + p % 8))
    return lax.ppermute(x, AXES, pairs)


def to_core(x):
    return send(x, lambda i, o: (i ^ 1, o))


def to_x(x):
    return send(x, lambda i, o: (i ^ 2, o))


def up(x):
    return send(x, lambda i, o: (i, o + 1))


def down(x):
    return send(x, lambda i, o: (i, o - 1))


def local(queries, keys, values, block_chain, block_depth):
    kv = pack(keys, values)
    half = kv.shape[0]
    pair = jnp.concatenate([kv, to_x(kv)], axis=0)
    stages = [[(0, 0), (2, 0), (1, 0), (3, 0)]]
    for d in (1, 2, 3):
        stages.append([(f, sign * d) for sign in (-1, 1) for f in (0, 2, 1, 3)])
    stages.append([(f, 4) for f in (0, 1, 2, 3)])
    run = functools.partial(attend, queries, block_chain, block_depth, stages)
    rising = falling = pair
    arrays, state = [pair, to_core(pair)], None
    for d in range(4):
        if d < 3:
            rising, falling = up(rising), down(falling)
        else:
            rising, falling = up(rising[:half]), down(falling[half:])
        state = run(d, arrays, state)
        rising, falling, state = lax.optimization_barrier((rising, falling, state))
        arrays = [rising, to_core(rising), falling, to_core(falling)]
    return run(4, arrays, state)


def solution(mesh):
    return jax.shard_map(
        local,
        mesh=mesh,
        in_specs=(
            P(("inner", "outer"), "heads"),
            P(("inner", "outer"), "heads"),
            P(("inner", "outer"), "heads"),
            P(),
            P(),
        ),
        out_specs=P(("inner", "outer"), "heads"),
        check_vma=False,
    )
```

```python
import functools
import math

import jax
import jax.numpy as jnp
from jax import lax
from jax.experimental import pallas as pl
from jax.experimental.pallas import tpu as pltpu
from jax.sharding import PartitionSpec as P

BLOCK = 128
HEAD = 128
TILE = 4
UNIT = 4 * BLOCK
LOWEST = -1e30
AXES = ("inner", "outer")


def dot(a, b, contract):
    return lax.dot_general(a, b, (contract, ((), ())), preferred_element_type=jnp.float32)


def in_hbm(x):
    return pltpu.with_memory_space_constraint(x, pltpu.HBM)


def plan_order(chain_ref, depth_ref, order, stages):
    inner = lax.axis_index("inner")
    outer = lax.axis_index("outer")
    q_chain, q_depth, counts = [], [], []
    for qb in range(2):
        own = (inner * 8 + outer) * 2 + qb
        q_chain.append(chain_ref[own])
        q_depth.append(depth_ref[own])
        counts.append(jnp.int32(0))
    row = 0
    for j, pieces in enumerate(stages):
        for flip, offset in pieces:
            source = (jnp.bitwise_xor(inner, flip) * 8 + lax.rem(outer + offset + 8, 8)) * 2
            for b in range(2):
                chain = chain_ref[source + b]
                depth = depth_ref[source + b]
                for qb in range(2):
                    seen = ((chain == 0) | (chain == q_chain[qb])) & (depth < q_depth[qb])
                    order[qb, counts[qb]] = row + b * BLOCK
                    counts[qb] = counts[qb] + seen.astype(jnp.int32)
            row += UNIT
        for qb in range(2):
            order[qb, 64 + j] = counts[qb]


def attend_kernel(*refs, stage, stages, start, count_in, heads):
    first, final = stage == 0, stage == len(stages) - 1
    refs = list(refs)
    if first:
        chain_hbm, depth_hbm, q_hbm = refs[:3]
        piece_refs = refs[3: 3 + count_in]
        kv_buf, shift, acc, q_ref, order, chain_ref, depth_ref, sem, table_sem, q_sem = refs[3 + count_in:]
    else:
        order = refs[0]
        piece_refs = refs[1: 1 + count_in]
        q_ref = refs[1 + count_in]
        refs = refs[5 + count_in:]
        if final:
            o_ref = refs.pop(0)
        kv_buf, shift, acc, sem = refs
    copies = []
    for ref in piece_refs:
        rows = ref.shape[0]
        copies.append(pltpu.make_async_copy(ref, kv_buf.at[pl.ds(start, rows), :], sem))
        start += rows
    if first:
        tables = [
            pltpu.make_async_copy(chain_hbm, chain_ref, table_sem.at[0]),
            pltpu.make_async_copy(depth_hbm, depth_ref, table_sem.at[1]),
        ]
        copies.append(pltpu.make_async_copy(q_hbm, q_ref, q_sem))
        for copy in tables + copies:
            copy.start()
        for copy in tables:
            copy.wait()
        plan_order(chain_ref, depth_ref, order, stages)
    else:
        for copy in copies:
            copy.start()
    for copy in copies:
        copy.wait()
    scale = HEAD ** -0.5 * math.log2(math.e)
    width = heads * BLOCK

    def heads_of(qb):
        rows = pl.ds(pl.multiple_of(qb * BLOCK, BLOCK), BLOCK)
        return jnp.concatenate([q_ref[rows, h * HEAD:(h + 1) * HEAD] for h in range(heads)], axis=0)

    def keys_of(row):
        return kv_buf[pl.ds(pl.multiple_of(row, BLOCK), BLOCK), :]

    def values_of(row):
        return kv_buf[pl.ds(pl.multiple_of(row + 2 * BLOCK, BLOCK), BLOCK), :]

    def with_ones(v):
        return jnp.concatenate([v, jnp.ones((16, v.shape[1]), v.dtype)], axis=0)

    def diagonal(qb):
        row = qb * BLOCK
        s = dot(keys_of(row), heads_of(qb), ((1,), (1,)))
        key = lax.broadcasted_iota(jnp.int32, s.shape, 0)
        query = lax.broadcasted_iota(jnp.int32, s.shape, 1)
        s = jnp.where(key <= lax.rem(query, BLOCK), s, LOWEST)
        top = jnp.max(s, axis=0, keepdims=True)
        weights = jnp.exp2((s - top) * scale).astype(jnp.bfloat16)
        shift[qb] = top
        acc[qb] = dot(with_ones(values_of(row)), weights, ((1,), (0,)))

    def tile_of(qb, at, left):
        rows = [order[qb, at]]
        rows += [jnp.where(i < left, order[qb, at + i], rows[0]) for i in range(1, TILE)]
        k = jnp.concatenate([keys_of(r) for r in rows], axis=0)
        v = with_ones(jnp.concatenate([values_of(r) for r in rows], axis=1))
        col = lax.broadcasted_iota(jnp.int32, v.shape, 1)
        v = jnp.where(col < left * BLOCK, v, jnp.zeros_like(v))
        return k, v

    def fast_tile(qb, at, left):
        k, v = tile_of(qb, at, left)
        s = dot(k, heads_of(qb), ((1,), (1,)))
        weights = jnp.exp2((s - shift[qb]) * scale).astype(jnp.bfloat16)
        acc[qb] += dot(v, weights, ((1,), (0,)))

    def safe_tile(qb, at, left):
        k, v = tile_of(qb, at, left)
        s = dot(k, heads_of(qb), ((1,), (1,)))
        before = shift[qb]
        after = jnp.maximum(before, jnp.max(s, axis=0, keepdims=True))
        weights = jnp.exp2((s - after) * scale).astype(jnp.bfloat16)
        shift[qb] = after
        acc[qb] = acc[qb] * jnp.exp2((before - after) * scale) + dot(v, weights, ((1,), (0,)))

    def one_block(qb, _):
        if first:
            diagonal(qb)
            done = 0
        else:
            done = lax.div(order[qb, 64 + stage - 1], TILE)
        now = order[qb, 64 + stage]
        until = lax.div(now + TILE - 1, TILE) if final else lax.div(now, TILE)

        def step(t, _):
            fast_tile(qb, t * TILE, now - t * TILE)
            return 0

        lax.fori_loop(done, until, step, 0)
        if final:
            total = acc[qb, HEAD:HEAD + 1, :]
            fine = jnp.min(jnp.where(total < 2.0 ** 64, 1.0, 0.0))

            @pl.when(fine < 0.5)
            def _():
                diagonal(qb)

                def again(t, _):
                    safe_tile(qb, t * TILE, now - t * TILE)
                    return 0

                lax.fori_loop(0, until, again, 0)

            mixed = acc[qb, :HEAD, :] / acc[qb, HEAD:HEAD + 1, :]
            rows = pl.ds(pl.multiple_of(qb * BLOCK, BLOCK), BLOCK)
            for h in range(heads):
                part = mixed[:, h * BLOCK:(h + 1) * BLOCK]
                o_ref[rows, h * HEAD:(h + 1) * HEAD] = part.T.astype(jnp.bfloat16)
        return 0

    lax.fori_loop(0, 2, one_block, 0)


def attend(queries, chain, depth, stages, stage, arrays, state):
    rows, width = queries.shape
    heads = width // HEAD
    first, final = stage == 0, stage == len(stages) - 1
    vmem = pl.BlockSpec(memory_space=pltpu.VMEM)
    smem = pl.BlockSpec(memory_space=pltpu.SMEM)
    anywhere = pl.BlockSpec(memory_space=pl.ANY)
    hbm = pl.BlockSpec(memory_space=pltpu.HBM)
    units = sum(len(p) for p in stages)
    start = UNIT * sum(len(p) for p in stages[:stage])
    held = [
        pltpu.VMEM((units * UNIT, HEAD), jnp.bfloat16),
        pltpu.VMEM((2, 1, heads * BLOCK), jnp.float32),
        pltpu.VMEM((2, HEAD + 16, heads * BLOCK), jnp.float32),
    ]
    out = jax.ShapeDtypeStruct((rows, width), jnp.bfloat16)
    n = len(arrays)
    body = functools.partial(
        attend_kernel, stage=stage, stages=stages, start=start, count_in=n, heads=heads
    )
    params = pltpu.CompilerParams(vmem_limit_bytes=32 << 20)
    sem = pltpu.SemaphoreType.DMA(())
    pairs = len(stages[stage]) * 2
    cost = pl.CostEstimate(
        flops=pairs * 4 * heads * BLOCK * BLOCK * HEAD,
        transcendentals=pairs * heads * BLOCK * BLOCK,
        bytes_accessed=pairs * BLOCK * HEAD * 4 + rows * width * 2,
    )
    if first:
        blocks = chain.shape[0]
        return pl.pallas_call(
            body,
            out_shape=held
            + [pltpu.VMEM((rows, width), jnp.bfloat16), jax.ShapeDtypeStruct((2, 128), jnp.int32)],
            in_specs=[hbm] * 3 + [anywhere] * n,
            out_specs=[vmem] * 4 + [smem],
            scratch_shapes=[
                pltpu.SMEM((blocks,), jnp.int32),
                pltpu.SMEM((blocks,), jnp.int32),
                sem,
                pltpu.SemaphoreType.DMA((2,)),
                sem,
            ],
            compiler_params=params,
            cost_estimate=cost,
            name="attend_first",
        )(*(in_hbm(x) for x in (chain, depth, queries)), *arrays)
    kv_buf, shift, acc, q_held, order = state
    result = pl.pallas_call(
        body,
        out_shape=([out] if final else []) + held,
        in_specs=[smem] + [anywhere] * n + [vmem] * 4,
        out_specs=[vmem] * (4 if final else 3),
        input_output_aliases={2 + n + i: i + final for i in range(3)},
        scratch_shapes=[sem],
        compiler_params=params,
        cost_estimate=cost,
        name="attend_last" if final else "attend_next",
    )(order, *arrays, q_held, kv_buf, shift, acc)
    return result[0] if final else (*result, q_held, order)


def pack_kernel(k_ref, v_ref, o_ref):
    for b in range(2):
        rows = slice(b * BLOCK, (b + 1) * BLOCK)
        o_ref[b * BLOCK:(b + 1) * BLOCK, :] = k_ref[rows, :]
        o_ref[(2 + b) * BLOCK:(3 + b) * BLOCK, :] = v_ref[rows, :].T


def pack(keys, values):
    vmem = pl.BlockSpec(memory_space=pltpu.VMEM)
    return pl.pallas_call(
        pack_kernel,
        out_shape=pltpu.VMEM((UNIT, HEAD), keys.dtype),
        in_specs=[vmem, vmem],
        out_specs=vmem,
        name="pack",
    )(keys, values)


def send(x, route):
    pairs = []
    for i in range(4):
        for o in range(8):
            j, p = route(i, o)
            pairs.append((i * 8 + o, j * 8 + p % 8))
    return lax.ppermute(x, AXES, pairs)


def to_core(x):
    return send(x, lambda i, o: (i ^ 1, o))


def to_x(x):
    return send(x, lambda i, o: (i ^ 2, o))


def up(x):
    return send(x, lambda i, o: (i, o + 1))


def down(x):
    return send(x, lambda i, o: (i, o - 1))


def local(queries, keys, values, block_chain, block_depth):
    unit = pack(keys, values)
    stages = [[(0, 0)], [(2, 0), (1, 0), (3, 0)]]
    for d in (1, 2, 3):
        stages.append([(f, sign * d) for sign in (-1, 1) for f in (0, 2, 1, 3)])
    stages.append([(f, 4) for f in (0, 1, 2, 3)])
    run = functools.partial(attend, queries, block_chain, block_depth, stages)
    across = to_x(unit)
    state = run(0, [unit], None)
    across, state = lax.optimization_barrier((across, state))
    pair = jnp.concatenate([unit, across], axis=0)
    rising = falling = pair
    arrays = [across, to_core(pair)]
    for d in range(1, 5):
        if d < 4:
            rising, falling = up(rising), down(falling)
        else:
            rising, falling = up(rising[:UNIT]), down(falling[UNIT:])
        state = run(d, arrays, state)
        rising, falling, state = lax.optimization_barrier((rising, falling, state))
        arrays = [rising, to_core(rising), falling, to_core(falling)]
    return run(5, arrays, state)


def solution(mesh):
    return jax.shard_map(
        local,
        mesh=mesh,
        in_specs=(
            P(("inner", "outer"), "heads"),
            P(("inner", "outer"), "heads"),
            P(("inner", "outer"), "heads"),
            P(),
            P(),
        ),
        out_specs=P(("inner", "outer"), "heads"),
        check_vma=False,
    )
```

```python
import functools
import math

import jax
import jax.numpy as jnp
from jax import lax
from jax.experimental import pallas as pl
from jax.experimental.pallas import tpu as pltpu
from jax.sharding import PartitionSpec as P

BLOCK = 128
HEAD = 128
TILE = 4
UNIT = 4 * BLOCK
LOWEST = -1e30
AXES = ("inner", "outer")


def dot(a, b, contract):
    return lax.dot_general(a, b, (contract, ((), ())), preferred_element_type=jnp.float32)


def in_hbm(x):
    return pltpu.with_memory_space_constraint(x, pltpu.HBM)


def plan_order(chain_ref, depth_ref, order, stages):
    inner = lax.axis_index("inner")
    outer = lax.axis_index("outer")
    core = jnp.bitwise_and(inner, 1)
    q_chain, q_depth, counts = [], [], []
    for qb in range(2):
        own = (inner * 8 + outer) * 2 + qb
        q_chain.append(chain_ref[own])
        q_depth.append(depth_ref[own])
        counts.append(jnp.int32(0))
    row = 0
    for j, pieces in enumerate(stages):
        for flip, even, odd in pieces:
            offset = even + core * (odd - even)
            source = (jnp.bitwise_xor(inner, flip) * 8 + lax.rem(outer + offset + 8, 8)) * 2
            for b in range(2):
                chain = chain_ref[source + b]
                depth = depth_ref[source + b]
                for qb in range(2):
                    seen = ((chain == 0) | (chain == q_chain[qb])) & (depth < q_depth[qb])
                    order[qb, counts[qb]] = row + b * BLOCK
                    counts[qb] = counts[qb] + seen.astype(jnp.int32)
            row += UNIT
        for qb in range(2):
            order[qb, 64 + j] = counts[qb]


def attend_kernel(*refs, stage, stages, start, count_in, heads):
    first, final = stage == 0, stage == len(stages) - 1
    refs = list(refs)
    if first:
        chain_hbm, depth_hbm, q_hbm = refs[:3]
        piece_refs = refs[3: 3 + count_in]
        kv_buf, shift, acc, q_ref, order, chain_ref, depth_ref, sem, table_sem, q_sem = refs[3 + count_in:]
    else:
        order = refs[0]
        piece_refs = refs[1: 1 + count_in]
        q_ref = refs[1 + count_in]
        refs = refs[5 + count_in:]
        if final:
            o_ref = refs.pop(0)
        kv_buf, shift, acc, sem = refs
    copies = []
    for ref in piece_refs:
        rows = ref.shape[0]
        copies.append(pltpu.make_async_copy(ref, kv_buf.at[pl.ds(start, rows), :], sem))
        start += rows
    if first:
        tables = [
            pltpu.make_async_copy(chain_hbm, chain_ref, table_sem.at[0]),
            pltpu.make_async_copy(depth_hbm, depth_ref, table_sem.at[1]),
        ]
        copies.append(pltpu.make_async_copy(q_hbm, q_ref, q_sem))
        for copy in tables + copies:
            copy.start()
        for copy in tables:
            copy.wait()
        plan_order(chain_ref, depth_ref, order, stages)
    else:
        for copy in copies:
            copy.start()
    for copy in copies:
        copy.wait()
    scale = HEAD ** -0.5 * math.log2(math.e)
    width = heads * BLOCK

    def heads_of(qb):
        rows = pl.ds(pl.multiple_of(qb * BLOCK, BLOCK), BLOCK)
        return jnp.concatenate([q_ref[rows, h * HEAD:(h + 1) * HEAD] for h in range(heads)], axis=0)

    def keys_of(row):
        return kv_buf[pl.ds(pl.multiple_of(row, BLOCK), BLOCK), :]

    def values_of(row):
        return kv_buf[pl.ds(pl.multiple_of(row + 2 * BLOCK, BLOCK), BLOCK), :]

    def with_ones(v):
        return jnp.concatenate([v, jnp.ones((16, v.shape[1]), v.dtype)], axis=0)

    def diagonal(qb):
        row = qb * BLOCK
        s = dot(keys_of(row), heads_of(qb), ((1,), (1,)))
        key = lax.broadcasted_iota(jnp.int32, s.shape, 0)
        query = lax.broadcasted_iota(jnp.int32, s.shape, 1)
        s = jnp.where(key <= lax.rem(query, BLOCK), s, LOWEST)
        top = jnp.max(s, axis=0, keepdims=True)
        weights = jnp.exp2((s - top) * scale).astype(jnp.bfloat16)
        shift[qb] = top
        acc[qb] = dot(with_ones(values_of(row)), weights, ((1,), (0,)))

    def tile_of(qb, at, left):
        rows = [order[qb, at]]
        rows += [jnp.where(i < left, order[qb, at + i], rows[0]) for i in range(1, TILE)]
        k = jnp.concatenate([keys_of(r) for r in rows], axis=0)
        v = with_ones(jnp.concatenate([values_of(r) for r in rows], axis=1))
        col = lax.broadcasted_iota(jnp.int32, v.shape, 1)
        v = jnp.where(col < left * BLOCK, v, jnp.zeros_like(v))
        return k, v

    def fast_tile(qb, at, left):
        k, v = tile_of(qb, at, left)
        s = dot(k, heads_of(qb), ((1,), (1,)))
        weights = jnp.exp2((s - shift[qb]) * scale).astype(jnp.bfloat16)
        acc[qb] += dot(v, weights, ((1,), (0,)))

    def safe_tile(qb, at, left):
        k, v = tile_of(qb, at, left)
        s = dot(k, heads_of(qb), ((1,), (1,)))
        before = shift[qb]
        after = jnp.maximum(before, jnp.max(s, axis=0, keepdims=True))
        weights = jnp.exp2((s - after) * scale).astype(jnp.bfloat16)
        shift[qb] = after
        acc[qb] = acc[qb] * jnp.exp2((before - after) * scale) + dot(v, weights, ((1,), (0,)))

    def one_block(qb, _):
        if first:
            diagonal(qb)
            done = 0
        else:
            done = lax.div(order[qb, 64 + stage - 1], TILE)
        now = order[qb, 64 + stage]
        until = lax.div(now + TILE - 1, TILE) if final else lax.div(now, TILE)

        def step(t, _):
            fast_tile(qb, t * TILE, now - t * TILE)
            return 0

        lax.fori_loop(done, until, step, 0)
        if final:
            total = acc[qb, HEAD:HEAD + 1, :]
            fine = jnp.min(jnp.where(total < 2.0 ** 64, 1.0, 0.0))

            @pl.when(fine < 0.5)
            def _():
                diagonal(qb)

                def again(t, _):
                    safe_tile(qb, t * TILE, now - t * TILE)
                    return 0

                lax.fori_loop(0, until, again, 0)

            mixed = acc[qb, :HEAD, :] / acc[qb, HEAD:HEAD + 1, :]
            rows = pl.ds(pl.multiple_of(qb * BLOCK, BLOCK), BLOCK)
            for h in range(heads):
                part = mixed[:, h * BLOCK:(h + 1) * BLOCK]
                o_ref[rows, h * HEAD:(h + 1) * HEAD] = part.T.astype(jnp.bfloat16)
        return 0

    lax.fori_loop(0, 2, one_block, 0)


def attend(queries, chain, depth, stages, stage, arrays, state):
    rows, width = queries.shape
    heads = width // HEAD
    first, final = stage == 0, stage == len(stages) - 1
    vmem = pl.BlockSpec(memory_space=pltpu.VMEM)
    smem = pl.BlockSpec(memory_space=pltpu.SMEM)
    anywhere = pl.BlockSpec(memory_space=pl.ANY)
    hbm = pl.BlockSpec(memory_space=pltpu.HBM)
    units = sum(len(p) for p in stages)
    start = UNIT * sum(len(p) for p in stages[:stage])
    held = [
        pltpu.VMEM((units * UNIT, HEAD), jnp.bfloat16),
        pltpu.VMEM((2, 1, heads * BLOCK), jnp.float32),
        pltpu.VMEM((2, HEAD + 16, heads * BLOCK), jnp.float32),
    ]
    out = jax.ShapeDtypeStruct((rows, width), jnp.bfloat16)
    n = len(arrays)
    body = functools.partial(
        attend_kernel, stage=stage, stages=stages, start=start, count_in=n, heads=heads
    )
    params = pltpu.CompilerParams(vmem_limit_bytes=32 << 20)
    sem = pltpu.SemaphoreType.DMA(())
    pairs = len(stages[stage]) * 2
    cost = pl.CostEstimate(
        flops=pairs * 4 * heads * BLOCK * BLOCK * HEAD,
        transcendentals=pairs * heads * BLOCK * BLOCK,
        bytes_accessed=pairs * BLOCK * HEAD * 4 + rows * width * 2,
    )
    if first:
        blocks = chain.shape[0]
        return pl.pallas_call(
            body,
            out_shape=held
            + [pltpu.VMEM((rows, width), jnp.bfloat16), jax.ShapeDtypeStruct((2, 128), jnp.int32)],
            in_specs=[hbm] * 3 + [anywhere] * n,
            out_specs=[vmem] * 4 + [smem],
            scratch_shapes=[
                pltpu.SMEM((blocks,), jnp.int32),
                pltpu.SMEM((blocks,), jnp.int32),
                sem,
                pltpu.SemaphoreType.DMA((2,)),
                sem,
            ],
            compiler_params=params,
            cost_estimate=cost,
            name="attend_first",
        )(*(in_hbm(x) for x in (chain, depth, queries)), *arrays)
    kv_buf, shift, acc, q_held, order = state
    result = pl.pallas_call(
        body,
        out_shape=([out] if final else []) + held,
        in_specs=[smem] + [anywhere] * n + [vmem] * 4,
        out_specs=[vmem] * (4 if final else 3),
        input_output_aliases={2 + n + i: i + final for i in range(3)},
        scratch_shapes=[sem],
        compiler_params=params,
        cost_estimate=cost,
        name="attend_last" if final else "attend_next",
    )(order, *arrays, q_held, kv_buf, shift, acc)
    return result[0] if final else (*result, q_held, order)


def pack_kernel(k_ref, v_ref, o_ref):
    for b in range(2):
        rows = slice(b * BLOCK, (b + 1) * BLOCK)
        o_ref[b * BLOCK:(b + 1) * BLOCK, :] = k_ref[rows, :]
        o_ref[(2 + b) * BLOCK:(3 + b) * BLOCK, :] = v_ref[rows, :].T


def pack(keys, values):
    vmem = pl.BlockSpec(memory_space=pltpu.VMEM)
    return pl.pallas_call(
        pack_kernel,
        out_shape=pltpu.VMEM((UNIT, HEAD), keys.dtype),
        in_specs=[vmem, vmem],
        out_specs=vmem,
        name="pack",
    )(keys, values)


def send(x, route):
    pairs = []
    for i in range(4):
        for o in range(8):
            j, p = route(i, o)
            pairs.append((i * 8 + o, j * 8 + p % 8))
    return lax.ppermute(x, AXES, pairs)


def to_core(x):
    return send(x, lambda i, o: (i ^ 1, o))


def to_x(x):
    return send(x, lambda i, o: (i ^ 2, o))


def ring(x):
    return send(x, lambda i, o: (i, o - 1 if i % 2 else o + 1))


def local(queries, keys, values, block_chain, block_depth):
    unit = pack(keys, values)
    own = [[(f, -d, d) for f in (0, 1)] for d in range(5)]
    own_x = [[(f ^ 2, -d, d) for f in (0, 1)] for d in range(5)]
    other = [[(f ^ 1, d, -d) for f in (0, 1)] for d in range(5)]
    other_x = [[(f ^ 3, d, -d) for f in (0, 1)] for d in range(5)]
    stages = [
        own[0],
        own_x[0] + own[1],
        own[2] + own_x[1] + other[1],
        own[3] + own_x[2] + other[2] + other_x[1],
        own[4] + own_x[3] + other[3] + other_x[2],
        own_x[4] + other_x[3],
    ]
    run = functools.partial(attend, queries, block_chain, block_depth, stages)

    def meet(*xs):
        return lax.optimization_barrier(xs)

    r0 = jnp.concatenate([unit, to_core(unit)], axis=0)
    x0, r1 = to_x(r0), ring(r0)
    state = run(0, [r0], None)
    r1, state = meet(r1, state)
    x1, c1, r2 = to_x(r1), to_core(r1), ring(r1)
    state = run(1, [x0, r1], state)
    r2, state = meet(r2, state)
    x2, c2, r3, cx1 = to_x(r2), to_core(r2), ring(r2), to_core(x1)
    state = run(2, [r2, x1, c1], state)
    r3, state = meet(r3, state)
    x3, c3, r4, cx2 = to_x(r3), to_core(r3), ring(r3), to_core(x2)
    state = run(3, [r3, x2, c2, cx1], state)
    r4, state = meet(r4, state)
    x4, cx3 = to_x(r4), to_core(x3)
    state = run(4, [r4, x3, c3, cx2], state)
    return run(5, [x4, cx3], state)


def solution(mesh):
    return jax.shard_map(
        local,
        mesh=mesh,
        in_specs=(
            P(("inner", "outer"), "heads"),
            P(("inner", "outer"), "heads"),
            P(("inner", "outer"), "heads"),
            P(),
            P(),
        ),
        out_specs=P(("inner", "outer"), "heads"),
        check_vma=False,
    )
```

```python
import functools
import math

import jax
import jax.numpy as jnp
from jax import lax
from jax.experimental import pallas as pl
from jax.experimental.pallas import tpu as pltpu
from jax.sharding import PartitionSpec as P

BLOCK = 128
HEAD = 128
TILE = 4
UNIT = 4 * BLOCK
LOWEST = -1e30
AXES = ("inner", "outer")


def dot(a, b, contract):
    return lax.dot_general(a, b, (contract, ((), ())), preferred_element_type=jnp.float32)


def in_hbm(x):
    return pltpu.with_memory_space_constraint(x, pltpu.HBM)


def plan_order(chain_ref, depth_ref, order, stages):
    inner = lax.axis_index("inner")
    outer = lax.axis_index("outer")
    core = jnp.bitwise_and(inner, 1)
    q_chain, q_depth, counts = [], [], []
    for qb in range(2):
        own = (inner * 8 + outer) * 2 + qb
        q_chain.append(chain_ref[own])
        q_depth.append(depth_ref[own])
        counts.append(jnp.int32(0))
    row = 0
    for j, pieces in enumerate(stages):
        for flip, even, odd in pieces:
            offset = even + core * (odd - even)
            source = (jnp.bitwise_xor(inner, flip) * 8 + lax.rem(outer + offset + 8, 8)) * 2
            for b in range(2):
                chain = chain_ref[source + b]
                depth = depth_ref[source + b]
                for qb in range(2):
                    seen = ((chain == 0) | (chain == q_chain[qb])) & (depth < q_depth[qb])
                    order[qb, counts[qb]] = row + b * BLOCK
                    counts[qb] = counts[qb] + seen.astype(jnp.int32)
            row += UNIT
        for qb in range(2):
            order[qb, 64 + j] = counts[qb]


def attend_kernel(*refs, stage, stages, start, count_in, heads):
    first, final = stage == 0, stage == len(stages) - 1
    flushed = (len(stages) - 2, len(stages) - 1)
    refs = list(refs)
    if first:
        chain_hbm, depth_hbm, q_hbm = refs[:3]
        piece_refs = refs[3: 3 + count_in]
        kv_buf, shift, acc, q_ref, order, chain_ref, depth_ref, sem, table_sem, q_sem = refs[3 + count_in:]
    else:
        order = refs[0]
        piece_refs = refs[1: 1 + count_in]
        q_ref = refs[1 + count_in]
        refs = refs[5 + count_in:]
        if final:
            o_ref = refs.pop(0)
        kv_buf, shift, acc, sem = refs
    copies = []
    for ref in piece_refs:
        rows = ref.shape[0]
        copies.append(pltpu.make_async_copy(ref, kv_buf.at[pl.ds(start, rows), :], sem))
        start += rows
    if first:
        tables = [
            pltpu.make_async_copy(chain_hbm, chain_ref, table_sem.at[0]),
            pltpu.make_async_copy(depth_hbm, depth_ref, table_sem.at[1]),
        ]
        copies.append(pltpu.make_async_copy(q_hbm, q_ref, q_sem))
        for copy in tables + copies:
            copy.start()
        for copy in tables:
            copy.wait()
        plan_order(chain_ref, depth_ref, order, stages)
    else:
        for copy in copies:
            copy.start()
    for copy in copies:
        copy.wait()
    scale = HEAD ** -0.5 * math.log2(math.e)
    width = heads * BLOCK

    def heads_of(qb):
        rows = pl.ds(pl.multiple_of(qb * BLOCK, BLOCK), BLOCK)
        return jnp.concatenate([q_ref[rows, h * HEAD:(h + 1) * HEAD] for h in range(heads)], axis=0)

    def keys_of(row):
        return kv_buf[pl.ds(pl.multiple_of(row, BLOCK), BLOCK), :]

    def values_of(row):
        return kv_buf[pl.ds(pl.multiple_of(row + 2 * BLOCK, BLOCK), BLOCK), :]

    def with_ones(v):
        return jnp.concatenate([v, jnp.ones((16, v.shape[1]), v.dtype)], axis=0)

    def diagonal(qb):
        row = qb * BLOCK
        s = dot(keys_of(row), heads_of(qb), ((1,), (1,)))
        key = lax.broadcasted_iota(jnp.int32, s.shape, 0)
        query = lax.broadcasted_iota(jnp.int32, s.shape, 1)
        s = jnp.where(key <= lax.rem(query, BLOCK), s, LOWEST)
        top = jnp.max(s, axis=0, keepdims=True)
        weights = jnp.exp2((s - top) * scale).astype(jnp.bfloat16)
        shift[qb] = top
        acc[qb] = dot(with_ones(values_of(row)), weights, ((1,), (0,)))

    def tile_of(qb, at, left, size):
        rows = [order[qb, at]]
        rows += [jnp.where(i < left, order[qb, at + i], rows[0]) for i in range(1, size)]
        k = jnp.concatenate([keys_of(r) for r in rows], axis=0)
        v = with_ones(jnp.concatenate([values_of(r) for r in rows], axis=1))
        col = lax.broadcasted_iota(jnp.int32, v.shape, 1)
        v = jnp.where(col < left * BLOCK, v, jnp.zeros_like(v))
        return k, v

    def fast_tile(qb, at, left, size=TILE):
        k, v = tile_of(qb, at, left, size)
        s = dot(k, heads_of(qb), ((1,), (1,)))
        weights = jnp.exp2((s - shift[qb]) * scale).astype(jnp.bfloat16)
        acc[qb] += dot(v, weights, ((1,), (0,)))

    def safe_tile(qb, at, left):
        k, v = tile_of(qb, at, left, TILE)
        s = dot(k, heads_of(qb), ((1,), (1,)))
        before = shift[qb]
        after = jnp.maximum(before, jnp.max(s, axis=0, keepdims=True))
        weights = jnp.exp2((s - after) * scale).astype(jnp.bfloat16)
        shift[qb] = after
        acc[qb] = acc[qb] * jnp.exp2((before - after) * scale) + dot(v, weights, ((1,), (0,)))

    def one_block(qb, _):
        now = order[qb, 64 + stage]
        if first:
            diagonal(qb)
            done = 0
        else:
            done = order[qb, 64 + stage - 1]
            if stage - 1 not in flushed:
                done = lax.div(done, TILE) * TILE
        full = lax.div(now - done, TILE)

        def step(t, _):
            fast_tile(qb, done + t * TILE, TILE)
            return 0

        lax.fori_loop(0, full, step, 0)
        if stage in flushed:
            at = done + full * TILE
            for size, wanted in ((2, now - at <= 2), (TILE, now - at > 2)):

                @pl.when((now > at) & wanted)
                def _():
                    fast_tile(qb, at, now - at, size)

        if final:
            total = acc[qb, HEAD:HEAD + 1, :]
            fine = jnp.min(jnp.where(total < 2.0 ** 64, 1.0, 0.0))

            @pl.when(fine < 0.5)
            def _():
                diagonal(qb)

                def again(t, _):
                    safe_tile(qb, t * TILE, now - t * TILE)
                    return 0

                lax.fori_loop(0, lax.div(now + TILE - 1, TILE), again, 0)

            inverse = 1.0 / acc[qb, HEAD:HEAD + 1, :]
            mixed = (acc[qb, :HEAD, :] * inverse).astype(jnp.bfloat16)
            rows = pl.ds(pl.multiple_of(qb * BLOCK, BLOCK), BLOCK)
            for h in range(heads):
                part = mixed[:, h * BLOCK:(h + 1) * BLOCK]
                o_ref[rows, h * HEAD:(h + 1) * HEAD] = part.T
        return 0

    lax.fori_loop(0, 2, one_block, 0)


def attend(queries, chain, depth, stages, stage, arrays, state):
    rows, width = queries.shape
    heads = width // HEAD
    first, final = stage == 0, stage == len(stages) - 1
    vmem = pl.BlockSpec(memory_space=pltpu.VMEM)
    smem = pl.BlockSpec(memory_space=pltpu.SMEM)
    anywhere = pl.BlockSpec(memory_space=pl.ANY)
    hbm = pl.BlockSpec(memory_space=pltpu.HBM)
    units = sum(len(p) for p in stages)
    start = UNIT * sum(len(p) for p in stages[:stage])
    held = [
        pltpu.VMEM((units * UNIT, HEAD), jnp.bfloat16),
        pltpu.VMEM((2, 1, heads * BLOCK), jnp.float32),
        pltpu.VMEM((2, HEAD + 16, heads * BLOCK), jnp.float32),
    ]
    out = jax.ShapeDtypeStruct((rows, width), jnp.bfloat16)
    n = len(arrays)
    body = functools.partial(
        attend_kernel, stage=stage, stages=stages, start=start, count_in=n, heads=heads
    )
    params = pltpu.CompilerParams(vmem_limit_bytes=32 << 20)
    sem = pltpu.SemaphoreType.DMA(())
    pairs = len(stages[stage]) * 2
    cost = pl.CostEstimate(
        flops=pairs * 4 * heads * BLOCK * BLOCK * HEAD,
        transcendentals=pairs * heads * BLOCK * BLOCK,
        bytes_accessed=pairs * BLOCK * HEAD * 4 + rows * width * 2,
    )
    if first:
        blocks = chain.shape[0]
        return pl.pallas_call(
            body,
            out_shape=held
            + [pltpu.VMEM((rows, width), jnp.bfloat16), jax.ShapeDtypeStruct((2, 128), jnp.int32)],
            in_specs=[hbm] * 3 + [anywhere] * n,
            out_specs=[vmem] * 4 + [smem],
            scratch_shapes=[
                pltpu.SMEM((blocks,), jnp.int32),
                pltpu.SMEM((blocks,), jnp.int32),
                sem,
                pltpu.SemaphoreType.DMA((2,)),
                sem,
            ],
            compiler_params=params,
            cost_estimate=cost,
            name="attend_first",
        )(*(in_hbm(x) for x in (chain, depth, queries)), *arrays)
    kv_buf, shift, acc, q_held, order = state
    result = pl.pallas_call(
        body,
        out_shape=([out] if final else []) + held,
        in_specs=[smem] + [anywhere] * n + [vmem] * 4,
        out_specs=[vmem] * (4 if final else 3),
        input_output_aliases={2 + n + i: i + final for i in range(3)},
        scratch_shapes=[sem],
        compiler_params=params,
        cost_estimate=cost,
        name="attend_last" if final else "attend_next",
    )(order, *arrays, q_held, kv_buf, shift, acc)
    return result[0] if final else (*result, q_held, order)


def pack_kernel(k_ref, v_ref, o_ref):
    for b in range(2):
        rows = slice(b * BLOCK, (b + 1) * BLOCK)
        o_ref[b * BLOCK:(b + 1) * BLOCK, :] = k_ref[rows, :]
        o_ref[(2 + b) * BLOCK:(3 + b) * BLOCK, :] = v_ref[rows, :].T


def pack(keys, values):
    vmem = pl.BlockSpec(memory_space=pltpu.VMEM)
    return pl.pallas_call(
        pack_kernel,
        out_shape=pltpu.VMEM((UNIT, HEAD), keys.dtype),
        in_specs=[vmem, vmem],
        out_specs=vmem,
        name="pack",
    )(keys, values)


def send(x, route):
    pairs = []
    for i in range(4):
        for o in range(8):
            j, p = route(i, o)
            pairs.append((i * 8 + o, j * 8 + p % 8))
    return lax.ppermute(x, AXES, pairs)


def to_core(x):
    return send(x, lambda i, o: (i ^ 1, o))


def to_x(x):
    return send(x, lambda i, o: (i ^ 2, o))


def ring(x):
    return send(x, lambda i, o: (i, o - 1 if i % 2 else o + 1))


def local(queries, keys, values, block_chain, block_depth):
    unit = pack(keys, values)
    own = [[(f, -d, d) for f in (0, 1)] for d in range(5)]
    own_x = [[(f ^ 2, -d, d) for f in (0, 1)] for d in range(5)]
    other = [[(f ^ 1, d, -d) for f in (0, 1)] for d in range(5)]
    other_x = [[(f ^ 3, d, -d) for f in (0, 1)] for d in range(5)]
    stages = [
        own[0],
        own_x[0] + own[1],
        own[2] + own_x[1] + other[1],
        own[3] + own_x[2] + other[2] + other_x[1],
        own[4] + own_x[3] + other[3] + other_x[2],
        other_x[3],
        own_x[4],
    ]
    run = functools.partial(attend, queries, block_chain, block_depth, stages)

    def meet(*xs):
        return lax.optimization_barrier(xs)

    r0 = jnp.concatenate([unit, to_core(unit)], axis=0)
    x0, r1 = to_x(r0), ring(r0)
    state = run(0, [r0], None)
    r1, state = meet(r1, state)
    x1, c1, r2 = to_x(r1), to_core(r1), ring(r1)
    state = run(1, [x0, r1], state)
    r2, state = meet(r2, state)
    x2, c2, r3, cx1 = to_x(r2), to_core(r2), ring(r2), to_core(x1)
    state = run(2, [r2, x1, c1], state)
    r3, state = meet(r3, state)
    x3, c3, r4, cx2 = to_x(r3), to_core(r3), ring(r3), to_core(x2)
    state = run(3, [r3, x2, c2, cx1], state)
    r4, x3, state = meet(r4, x3, state)
    x4, cx3 = to_x(r4), to_core(x3)
    state = run(4, [r4, x3, c3, cx2], state)
    state = run(5, [cx3], state)
    return run(6, [x4], state)


def solution(mesh):
    return jax.shard_map(
        local,
        mesh=mesh,
        in_specs=(
            P(("inner", "outer"), "heads"),
            P(("inner", "outer"), "heads"),
            P(("inner", "outer"), "heads"),
            P(),
            P(),
        ),
        out_specs=P(("inner", "outer"), "heads"),
        check_vma=False,
    )
```

```python
import functools
import math

import jax
import jax.numpy as jnp
from jax import lax
from jax.experimental import pallas as pl
from jax.experimental.pallas import tpu as pltpu
from jax.sharding import PartitionSpec as P

BLOCK = 128
HEAD = 128
TILE = 4
UNIT = 4 * BLOCK
LOWEST = -1e30
AXES = ("inner", "outer")


def dot(a, b, contract):
    return lax.dot_general(a, b, (contract, ((), ())), preferred_element_type=jnp.float32)


def in_hbm(x):
    return pltpu.with_memory_space_constraint(x, pltpu.HBM)


def plan_order(chain_ref, depth_ref, order, stages):
    inner = lax.axis_index("inner")
    outer = lax.axis_index("outer")
    core = jnp.bitwise_and(inner, 1)
    q_chain, q_depth, counts = [], [], []
    for qb in range(2):
        own = (inner * 8 + outer) * 2 + qb
        q_chain.append(chain_ref[own])
        q_depth.append(depth_ref[own])
        counts.append(jnp.int32(0))
    row = 0
    for j, pieces in enumerate(stages):
        for flip, even, odd in pieces:
            offset = even + core * (odd - even)
            source = (jnp.bitwise_xor(inner, flip) * 8 + lax.rem(outer + offset + 8, 8)) * 2
            for b in range(2):
                chain = chain_ref[source + b]
                depth = depth_ref[source + b]
                for qb in range(2):
                    seen = ((chain == 0) | (chain == q_chain[qb])) & (depth < q_depth[qb])
                    order[qb, counts[qb]] = row + b * BLOCK
                    counts[qb] = counts[qb] + seen.astype(jnp.int32)
            row += UNIT
        for qb in range(2):
            order[qb, 64 + j] = counts[qb]


def attend_kernel(*refs, stage, stages, start, count_in, heads):
    first, final = stage == 0, stage == len(stages) - 1
    flushed = (len(stages) - 2, len(stages) - 1)
    refs = list(refs)
    if first:
        chain_hbm, depth_hbm, q_hbm = refs[:3]
        piece_refs = refs[3: 3 + count_in]
        kv_buf, shift, acc, q_ref, order, chain_ref, depth_ref, sem, table_sem, q_sem = refs[3 + count_in:]
    else:
        order = refs[0]
        piece_refs = refs[1: 1 + count_in]
        q_ref = refs[1 + count_in]
        refs = refs[5 + count_in:]
        if final:
            o_ref = refs.pop(0)
            out_buf, out_sem = refs[4:]
        kv_buf, shift, acc, sem = refs[:4]
    copies = []
    for ref in piece_refs:
        rows = ref.shape[0]
        copies.append(pltpu.make_async_copy(ref, kv_buf.at[pl.ds(start, rows), :], sem))
        start += rows
    if first:
        tables = [
            pltpu.make_async_copy(chain_hbm, chain_ref, table_sem.at[0]),
            pltpu.make_async_copy(depth_hbm, depth_ref, table_sem.at[1]),
        ]
        copies.append(pltpu.make_async_copy(q_hbm, q_ref, q_sem))
        for copy in tables + copies:
            copy.start()
        for copy in tables:
            copy.wait()
        plan_order(chain_ref, depth_ref, order, stages)
    else:
        for copy in copies:
            copy.start()
    for copy in copies:
        copy.wait()
    scale = HEAD ** -0.5 * math.log2(math.e)
    width = heads * BLOCK

    def heads_of(qb):
        rows = pl.ds(pl.multiple_of(qb * BLOCK, BLOCK), BLOCK)
        return jnp.concatenate([q_ref[rows, h * HEAD:(h + 1) * HEAD] for h in range(heads)], axis=0)

    def keys_of(row):
        return kv_buf[pl.ds(pl.multiple_of(row, BLOCK), BLOCK), :]

    def values_of(row):
        return kv_buf[pl.ds(pl.multiple_of(row + 2 * BLOCK, BLOCK), BLOCK), :]

    def with_ones(v):
        return jnp.concatenate([v, jnp.ones((16, v.shape[1]), v.dtype)], axis=0)

    def diagonal(qb):
        row = qb * BLOCK
        s = dot(keys_of(row), heads_of(qb), ((1,), (1,)))
        key = lax.broadcasted_iota(jnp.int32, s.shape, 0)
        query = lax.broadcasted_iota(jnp.int32, s.shape, 1)
        s = jnp.where(key <= lax.rem(query, BLOCK), s, LOWEST)
        top = jnp.max(s, axis=0, keepdims=True)
        weights = jnp.exp2((s - top) * scale).astype(jnp.bfloat16)
        shift[qb] = top
        acc[qb] = dot(with_ones(values_of(row)), weights, ((1,), (0,)))

    def tile_of(qb, at, left, size):
        rows = [order[qb, at]]
        rows += [jnp.where(i < left, order[qb, at + i], rows[0]) for i in range(1, size)]
        k = jnp.concatenate([keys_of(r) for r in rows], axis=0)
        v = with_ones(jnp.concatenate([values_of(r) for r in rows], axis=1))
        col = lax.broadcasted_iota(jnp.int32, v.shape, 1)
        v = jnp.where(col < left * BLOCK, v, jnp.zeros_like(v))
        return k, v

    def fast_tile(qb, at, left, size=TILE):
        k, v = tile_of(qb, at, left, size)
        s = dot(k, heads_of(qb), ((1,), (1,)))
        weights = jnp.exp2((s - shift[qb]) * scale).astype(jnp.bfloat16)
        acc[qb] += dot(v, weights, ((1,), (0,)))

    def safe_tile(qb, at, left):
        k, v = tile_of(qb, at, left, TILE)
        s = dot(k, heads_of(qb), ((1,), (1,)))
        before = shift[qb]
        after = jnp.maximum(before, jnp.max(s, axis=0, keepdims=True))
        weights = jnp.exp2((s - after) * scale).astype(jnp.bfloat16)
        shift[qb] = after
        acc[qb] = acc[qb] * jnp.exp2((before - after) * scale) + dot(v, weights, ((1,), (0,)))

    def out_copy(qb):
        rows = pl.ds(pl.multiple_of(qb * BLOCK, BLOCK), BLOCK)
        return pltpu.make_async_copy(out_buf.at[rows, :], o_ref.at[rows, :], out_sem.at[qb])

    def one_block(qb, _):
        now = order[qb, 64 + stage]
        if first:
            diagonal(qb)
            done = 0
        else:
            done = order[qb, 64 + stage - 1]
            if stage - 1 not in flushed:
                done = lax.div(done, TILE) * TILE
        full = lax.div(now - done, TILE)
        wide = lax.div(full, 2)

        def step(t, _):
            fast_tile(qb, done + t * 2 * TILE, 2 * TILE, 2 * TILE)
            return 0

        if len(stages[stage]) > 2:
            lax.fori_loop(0, wide, step, 0)

            @pl.when(full > 2 * wide)
            def _():
                fast_tile(qb, done + wide * 2 * TILE, TILE)

        elif not first:

            @pl.when(full > 0)
            def _():
                fast_tile(qb, done, TILE)

        if stage in flushed:
            at = done + full * TILE
            for size, wanted in ((2, now - at <= 2), (TILE, now - at > 2)):

                @pl.when((now > at) & wanted)
                def _():
                    fast_tile(qb, at, now - at, size)

        if final:
            total = acc[qb, HEAD:HEAD + 1, :]
            fine = jnp.min(jnp.where(total < 2.0 ** 64, 1.0, 0.0))

            @pl.when(fine < 0.5)
            def _():
                diagonal(qb)

                def again(t, _):
                    safe_tile(qb, t * TILE, now - t * TILE)
                    return 0

                lax.fori_loop(0, lax.div(now + TILE - 1, TILE), again, 0)

            inverse = 1.0 / acc[qb, HEAD:HEAD + 1, :]
            mixed = (acc[qb, :HEAD, :] * inverse).astype(jnp.bfloat16)
            rows = pl.ds(pl.multiple_of(qb * BLOCK, BLOCK), BLOCK)
            for h in range(heads):
                part = mixed[:, h * BLOCK:(h + 1) * BLOCK]
                out_buf[rows, h * HEAD:(h + 1) * HEAD] = part.T
            out_copy(qb).start()
        return 0

    lax.fori_loop(0, 2, one_block, 0)
    if final:
        for qb in range(2):
            out_copy(qb).wait()


def attend(queries, chain, depth, stages, stage, arrays, state):
    rows, width = queries.shape
    heads = width // HEAD
    first, final = stage == 0, stage == len(stages) - 1
    vmem = pl.BlockSpec(memory_space=pltpu.VMEM)
    smem = pl.BlockSpec(memory_space=pltpu.SMEM)
    anywhere = pl.BlockSpec(memory_space=pl.ANY)
    hbm = pl.BlockSpec(memory_space=pltpu.HBM)
    units = sum(len(p) for p in stages)
    start = UNIT * sum(len(p) for p in stages[:stage])
    held = [
        pltpu.VMEM((units * UNIT, HEAD), jnp.bfloat16),
        pltpu.VMEM((2, 1, heads * BLOCK), jnp.float32),
        pltpu.VMEM((2, HEAD + 16, heads * BLOCK), jnp.float32),
    ]
    out = jax.ShapeDtypeStruct((rows, width), jnp.bfloat16)
    n = len(arrays)
    body = functools.partial(
        attend_kernel, stage=stage, stages=stages, start=start, count_in=n, heads=heads
    )
    params = pltpu.CompilerParams(vmem_limit_bytes=32 << 20)
    sem = pltpu.SemaphoreType.DMA(())
    pairs = len(stages[stage]) * 2
    cost = pl.CostEstimate(
        flops=pairs * 4 * heads * BLOCK * BLOCK * HEAD,
        transcendentals=pairs * heads * BLOCK * BLOCK,
        bytes_accessed=pairs * BLOCK * HEAD * 4 + rows * width * 2,
    )
    if first:
        blocks = chain.shape[0]
        return pl.pallas_call(
            body,
            out_shape=held
            + [pltpu.VMEM((rows, width), jnp.bfloat16), jax.ShapeDtypeStruct((2, 128), jnp.int32)],
            in_specs=[hbm] * 3 + [anywhere] * n,
            out_specs=[vmem] * 4 + [smem],
            scratch_shapes=[
                pltpu.SMEM((blocks,), jnp.int32),
                pltpu.SMEM((blocks,), jnp.int32),
                sem,
                pltpu.SemaphoreType.DMA((2,)),
                sem,
            ],
            compiler_params=params,
            cost_estimate=cost,
            name="attend_first",
        )(*(in_hbm(x) for x in (chain, depth, queries)), *arrays)
    kv_buf, shift, acc, q_held, order = state
    result = pl.pallas_call(
        body,
        out_shape=([out] if final else []) + held,
        in_specs=[smem] + [anywhere] * n + [vmem] * 4,
        out_specs=([hbm] if final else []) + [vmem] * 3,
        input_output_aliases={2 + n + i: i + final for i in range(3)},
        scratch_shapes=[sem]
        + ([pltpu.VMEM(out.shape, out.dtype), pltpu.SemaphoreType.DMA((2,))] if final else []),
        compiler_params=params,
        cost_estimate=cost,
        name="attend_last" if final else "attend_next",
    )(order, *arrays, q_held, kv_buf, shift, acc)
    return result[0] if final else (*result, q_held, order)


def pack_kernel(k_ref, v_ref, o_ref):
    for b in range(2):
        rows = slice(b * BLOCK, (b + 1) * BLOCK)
        o_ref[b * BLOCK:(b + 1) * BLOCK, :] = k_ref[rows, :]
        o_ref[(2 + b) * BLOCK:(3 + b) * BLOCK, :] = v_ref[rows, :].T


def pack(keys, values):
    vmem = pl.BlockSpec(memory_space=pltpu.VMEM)
    return pl.pallas_call(
        pack_kernel,
        out_shape=pltpu.VMEM((UNIT, HEAD), keys.dtype),
        in_specs=[vmem, vmem],
        out_specs=vmem,
        name="pack",
    )(keys, values)


def send(x, route):
    pairs = []
    for i in range(4):
        for o in range(8):
            j, p = route(i, o)
            pairs.append((i * 8 + o, j * 8 + p % 8))
    return lax.ppermute(x, AXES, pairs)


def to_core(x):
    return send(x, lambda i, o: (i ^ 1, o))


def to_x(x):
    return send(x, lambda i, o: (i ^ 2, o))


def ring(x):
    return send(x, lambda i, o: (i, o - 1 if i % 2 else o + 1))


def local(queries, keys, values, block_chain, block_depth):
    unit = pack(keys, values)
    own = [[(f, -d, d) for f in (0, 1)] for d in range(5)]
    own_x = [[(f ^ 2, -d, d) for f in (0, 1)] for d in range(5)]
    other = [[(f ^ 1, d, -d) for f in (0, 1)] for d in range(5)]
    other_x = [[(f ^ 3, d, -d) for f in (0, 1)] for d in range(5)]
    stages = [
        own[0],
        own_x[0] + own[1],
        own[2] + own_x[1] + other[1],
        own[3] + own_x[2] + other[2] + other_x[1],
        own[4] + own_x[3] + other[3] + other_x[2],
        other_x[3],
        own_x[4],
    ]
    run = functools.partial(attend, queries, block_chain, block_depth, stages)

    def meet(*xs):
        return lax.optimization_barrier(xs)

    r0 = jnp.concatenate([unit, to_core(unit)], axis=0)
    x0, r1 = to_x(r0), ring(r0)
    state = run(0, [r0], None)
    r1, state = meet(r1, state)
    x1, c1, r2 = to_x(r1), to_core(r1), ring(r1)
    state = run(1, [x0, r1], state)
    r2, state = meet(r2, state)
    x2, c2, r3, cx1 = to_x(r2), to_core(r2), ring(r2), to_core(x1)
    state = run(2, [r2, x1, c1], state)
    r3, state = meet(r3, state)
    x3, c3, r4, cx2 = to_x(r3), to_core(r3), ring(r3), to_core(x2)
    state = run(3, [r3, x2, c2, cx1], state)
    r4, x3, state = meet(r4, x3, state)
    x4, cx3 = to_x(r4), to_core(x3)
    state = run(4, [r4, x3, c3, cx2], state)
    state = run(5, [cx3], state)
    return run(6, [x4], state)


def solution(mesh):
    return jax.shard_map(
        local,
        mesh=mesh,
        in_specs=(
            P(("inner", "outer"), "heads"),
            P(("inner", "outer"), "heads"),
            P(("inner", "outer"), "heads"),
            P(),
            P(),
        ),
        out_specs=P(("inner", "outer"), "heads"),
        check_vma=False,
    )
```

```python
import functools
import math

import jax
import jax.numpy as jnp
from jax import lax
from jax.experimental import pallas as pl
from jax.experimental.pallas import tpu as pltpu
from jax.sharding import PartitionSpec as P

BLOCK = 128
HEAD = 128
TILE = 4
UNIT = 4 * BLOCK
LOWEST = -1e30
AXES = ("inner", "outer")


def dot(a, b, contract):
    return lax.dot_general(a, b, (contract, ((), ())), preferred_element_type=jnp.float32)


def in_hbm(x):
    return pltpu.with_memory_space_constraint(x, pltpu.HBM)


def plan_order(chain_ref, depth_ref, order, stages):
    inner = lax.axis_index("inner")
    outer = lax.axis_index("outer")
    core = jnp.bitwise_and(inner, 1)
    q_chain, q_depth, counts = [], [], []
    for qb in range(2):
        own = (inner * 8 + outer) * 2 + qb
        q_chain.append(chain_ref[own])
        q_depth.append(depth_ref[own])
        counts.append(jnp.int32(0))
    row = 0
    for j, pieces in enumerate(stages):
        for flip, even, odd in pieces:
            offset = even + core * (odd - even)
            source = (jnp.bitwise_xor(inner, flip) * 8 + lax.rem(outer + offset + 8, 8)) * 2
            for b in range(2):
                chain = chain_ref[source + b]
                depth = depth_ref[source + b]
                for qb in range(2):
                    seen = ((chain == 0) | (chain == q_chain[qb])) & (depth < q_depth[qb])
                    order[qb, counts[qb]] = row + b * BLOCK
                    counts[qb] = counts[qb] + seen.astype(jnp.int32)
            row += UNIT
        for qb in range(2):
            order[qb, 64 + j] = counts[qb]


def attend_kernel(*refs, stage, stages, start, count_in, heads):
    first, final = stage == 0, stage == len(stages) - 1
    flushed = (len(stages) - 2, len(stages) - 1)
    refs = list(refs)
    if first:
        chain_hbm, depth_hbm, q_hbm = refs[:3]
        piece_refs = refs[3: 3 + count_in]
        kv_buf, shift, acc, q_ref, order, chain_ref, depth_ref, sem, table_sem, q_sem = refs[3 + count_in:]
    else:
        order = refs[0]
        piece_refs = refs[1: 1 + count_in]
        q_ref = refs[1 + count_in]
        refs = refs[5 + count_in:]
        if final:
            o_ref = refs.pop(0)
            out_buf, out_sem = refs[4:]
        kv_buf, shift, acc, sem = refs[:4]
    copies = []
    for ref in piece_refs:
        rows = ref.shape[0]
        copies.append(pltpu.make_async_copy(ref, kv_buf.at[pl.ds(start, rows), :], sem))
        start += rows
    if first:
        tables = [
            pltpu.make_async_copy(chain_hbm, chain_ref, table_sem.at[0]),
            pltpu.make_async_copy(depth_hbm, depth_ref, table_sem.at[1]),
        ]
        copies.append(pltpu.make_async_copy(q_hbm, q_ref, q_sem))
        for copy in tables + copies:
            copy.start()
        for copy in tables:
            copy.wait()
        plan_order(chain_ref, depth_ref, order, stages)
    else:
        for copy in copies:
            copy.start()
    for copy in copies:
        copy.wait()
    scale = HEAD ** -0.5 * math.log2(math.e)
    width = heads * BLOCK

    def heads_of(qb):
        rows = pl.ds(pl.multiple_of(qb * BLOCK, BLOCK), BLOCK)
        return jnp.concatenate([q_ref[rows, h * HEAD:(h + 1) * HEAD] for h in range(heads)], axis=0)

    def keys_of(row):
        return kv_buf[pl.ds(pl.multiple_of(row, BLOCK), BLOCK), :]

    def values_of(row):
        return kv_buf[pl.ds(pl.multiple_of(row + 2 * BLOCK, BLOCK), BLOCK), :]

    def with_ones(v):
        return jnp.concatenate([v, jnp.ones((16, v.shape[1]), v.dtype)], axis=0)

    def diagonal(qb):
        row = qb * BLOCK
        s = dot(keys_of(row), heads_of(qb), ((1,), (1,)))
        key = lax.broadcasted_iota(jnp.int32, s.shape, 0)
        query = lax.broadcasted_iota(jnp.int32, s.shape, 1)
        s = jnp.where(key <= lax.rem(query, BLOCK), s, LOWEST)
        top = jnp.max(s, axis=0, keepdims=True)
        weights = jnp.exp2((s - top) * scale).astype(jnp.bfloat16)
        shift[qb] = top
        acc[qb] = dot(with_ones(values_of(row)), weights, ((1,), (0,)))

    def tile_of(qb, at, left, size):
        rows = [order[qb, at]]
        rows += [jnp.where(i < left, order[qb, at + i], rows[0]) for i in range(1, size)]
        k = jnp.concatenate([keys_of(r) for r in rows], axis=0)
        v = with_ones(jnp.concatenate([values_of(r) for r in rows], axis=1))
        col = lax.broadcasted_iota(jnp.int32, v.shape, 1)
        v = jnp.where(col < left * BLOCK, v, jnp.zeros_like(v))
        return k, v

    def fast_tile(qb, at, left, size=TILE):
        k, v = tile_of(qb, at, left, size)
        s = dot(k, heads_of(qb), ((1,), (1,)))
        weights = jnp.exp2((s - shift[qb]) * scale).astype(jnp.bfloat16)
        acc[qb] += dot(v, weights, ((1,), (0,)))

    def safe_tile(qb, at, left):
        k, v = tile_of(qb, at, left, TILE)
        s = dot(k, heads_of(qb), ((1,), (1,)))
        before = shift[qb]
        after = jnp.maximum(before, jnp.max(s, axis=0, keepdims=True))
        weights = jnp.exp2((s - after) * scale).astype(jnp.bfloat16)
        shift[qb] = after
        acc[qb] = acc[qb] * jnp.exp2((before - after) * scale) + dot(v, weights, ((1,), (0,)))

    def out_copy(qb):
        rows = pl.ds(pl.multiple_of(qb * BLOCK, BLOCK), BLOCK)
        return pltpu.make_async_copy(out_buf.at[rows, :], o_ref.at[rows, :], out_sem.at[qb])

    def one_block(qb, _):
        now = order[qb, 64 + stage]
        if first:
            diagonal(qb)
            done = 0
        else:
            done = order[qb, 64 + stage - 1]
            if stage - 1 not in flushed:
                done = lax.div(done, TILE) * TILE
        full = lax.div(now - done, TILE)
        wide = lax.div(full, 2)

        def step(t, _):
            fast_tile(qb, done + t * 2 * TILE, 2 * TILE, 2 * TILE)
            return 0

        if len(stages[stage]) > 2:
            lax.fori_loop(0, wide, step, 0)

            @pl.when(full > 2 * wide)
            def _():
                fast_tile(qb, done + wide * 2 * TILE, TILE)

        elif not first:

            @pl.when(full > 0)
            def _():
                fast_tile(qb, done, TILE)

        if stage in flushed:
            at = done + full * TILE
            for size, wanted in ((2, now - at <= 2), (TILE, now - at > 2)):

                @pl.when((now > at) & wanted)
                def _():
                    fast_tile(qb, at, now - at, size)

        if final:
            total = acc[qb, HEAD:HEAD + 1, :]
            fine = jnp.min(jnp.where(total < 2.0 ** 64, 1.0, 0.0))

            @pl.when(fine < 0.5)
            def _():
                diagonal(qb)

                def again(t, _):
                    safe_tile(qb, t * TILE, now - t * TILE)
                    return 0

                lax.fori_loop(0, lax.div(now + TILE - 1, TILE), again, 0)

            inverse = 1.0 / acc[qb, HEAD:HEAD + 1, :]
            mixed = (acc[qb, :HEAD, :] * inverse).astype(jnp.bfloat16)
            rows = pl.ds(pl.multiple_of(qb * BLOCK, BLOCK), BLOCK)
            for h in range(heads):
                part = mixed[:, h * BLOCK:(h + 1) * BLOCK]
                out_buf[rows, h * HEAD:(h + 1) * HEAD] = part.T
            out_copy(qb).start()
        return 0

    lax.fori_loop(0, 2, one_block, 0)
    if final:
        for qb in range(2):
            out_copy(qb).wait()


def attend(queries, chain, depth, stages, stage, arrays, state):
    rows, width = queries.shape
    heads = width // HEAD
    first, final = stage == 0, stage == len(stages) - 1
    vmem = pl.BlockSpec(memory_space=pltpu.VMEM)
    smem = pl.BlockSpec(memory_space=pltpu.SMEM)
    anywhere = pl.BlockSpec(memory_space=pl.ANY)
    hbm = pl.BlockSpec(memory_space=pltpu.HBM)
    units = sum(len(p) for p in stages)
    start = UNIT * sum(len(p) for p in stages[:stage])
    held = [
        pltpu.VMEM((units * UNIT, HEAD), jnp.bfloat16),
        pltpu.VMEM((2, 1, heads * BLOCK), jnp.float32),
        pltpu.VMEM((2, HEAD + 16, heads * BLOCK), jnp.float32),
    ]
    out = jax.ShapeDtypeStruct((rows, width), jnp.bfloat16)
    n = len(arrays)
    body = functools.partial(
        attend_kernel, stage=stage, stages=stages, start=start, count_in=n, heads=heads
    )
    params = pltpu.CompilerParams(vmem_limit_bytes=32 << 20)
    sem = pltpu.SemaphoreType.DMA(())
    pairs = len(stages[stage]) * 2
    cost = pl.CostEstimate(
        flops=pairs * 4 * heads * BLOCK * BLOCK * HEAD,
        transcendentals=pairs * heads * BLOCK * BLOCK,
        bytes_accessed=pairs * BLOCK * HEAD * 4 + rows * width * 2,
    )
    if first:
        blocks = chain.shape[0]
        return pl.pallas_call(
            body,
            out_shape=held
            + [pltpu.VMEM((rows, width), jnp.bfloat16), jax.ShapeDtypeStruct((2, 128), jnp.int32)],
            in_specs=[hbm] * 3 + [anywhere] * n,
            out_specs=[vmem] * 4 + [smem],
            scratch_shapes=[
                pltpu.SMEM((blocks,), jnp.int32),
                pltpu.SMEM((blocks,), jnp.int32),
                sem,
                pltpu.SemaphoreType.DMA((2,)),
                sem,
            ],
            compiler_params=params,
            cost_estimate=cost,
            name="attend_first",
        )(*(in_hbm(x) for x in (chain, depth, queries)), *arrays)
    kv_buf, shift, acc, q_held, order = state
    result = pl.pallas_call(
        body,
        out_shape=([out] if final else []) + held,
        in_specs=[smem] + [anywhere] * n + [vmem] * 4,
        out_specs=([hbm] if final else []) + [vmem] * 3,
        input_output_aliases={2 + n + i: i + final for i in range(3)},
        scratch_shapes=[sem]
        + ([pltpu.VMEM(out.shape, out.dtype), pltpu.SemaphoreType.DMA((2,))] if final else []),
        compiler_params=params,
        cost_estimate=cost,
        name="attend_last" if final else "attend_next",
    )(order, *arrays, q_held, kv_buf, shift, acc)
    return result[0] if final else (*result, q_held, order)


def pack_kernel(k_ref, v_ref, o_ref):
    for b in range(2):
        rows = slice(b * BLOCK, (b + 1) * BLOCK)
        o_ref[b * BLOCK:(b + 1) * BLOCK, :] = k_ref[rows, :]
        o_ref[(2 + b) * BLOCK:(3 + b) * BLOCK, :] = v_ref[rows, :].T


def pack(keys, values):
    vmem = pl.BlockSpec(memory_space=pltpu.VMEM)
    return pl.pallas_call(
        pack_kernel,
        out_shape=pltpu.VMEM((UNIT, HEAD), keys.dtype),
        in_specs=[vmem, vmem],
        out_specs=vmem,
        name="pack",
    )(keys, values)


def send(x, route):
    pairs = []
    for i in range(4):
        for o in range(8):
            j, p = route(i, o)
            pairs.append((i * 8 + o, j * 8 + p % 8))
    return lax.ppermute(x, AXES, pairs)


def to_core(x):
    return send(x, lambda i, o: (i ^ 1, o))


def to_x(x):
    return send(x, lambda i, o: (i ^ 2, o))


def ring(x):
    return send(x, lambda i, o: (i, o - 1 if i % 2 else o + 1))


def local(queries, keys, values, block_chain, block_depth):
    unit = pack(keys, values)
    own = [[(f, -d, d) for f in (0, 1)] for d in range(5)]
    own_x = [[(f ^ 2, -d, d) for f in (0, 1)] for d in range(5)]
    other = [[(f ^ 1, d, -d) for f in (0, 1)] for d in range(5)]
    other_x = [[(f ^ 3, d, -d) for f in (0, 1)] for d in range(5)]
    stages = [
        own[0],
        own_x[0] + own[1] + other[1],
        own[2] + own_x[1] + other[2],
        own[3] + own_x[2] + other[3] + other_x[1],
        own[4] + own_x[3] + other_x[2],
        other_x[3],
        own_x[4],
    ]
    run = functools.partial(attend, queries, block_chain, block_depth, stages)

    def meet(*xs):
        return lax.optimization_barrier(xs)

    r0 = jnp.concatenate([unit, to_core(unit)], axis=0)
    x0, r1 = to_x(r0), ring(r0)
    state = run(0, [r0], None)
    r1, state = meet(r1, state)
    x1, c1, r2 = to_x(r1), to_core(r1), ring(r1)
    state = run(1, [x0, r1, c1], state)
    r2, state = meet(r2, state)
    x2, c2, r3, cx1 = to_x(r2), to_core(r2), ring(r2), to_core(x1)
    state = run(2, [r2, x1, c2], state)
    r3, state = meet(r3, state)
    x3, c3, r4, cx2 = to_x(r3), to_core(r3), ring(r3), to_core(x2)
    state = run(3, [r3, x2, c3, cx1], state)
    r4, x3, state = meet(r4, x3, state)
    x4, cx3 = to_x(r4), to_core(x3)
    state = run(4, [r4, x3, cx2], state)
    state = run(5, [cx3], state)
    return run(6, [x4], state)


def solution(mesh):
    return jax.shard_map(
        local,
        mesh=mesh,
        in_specs=(
            P(("inner", "outer"), "heads"),
            P(("inner", "outer"), "heads"),
            P(("inner", "outer"), "heads"),
            P(),
            P(),
        ),
        out_specs=P(("inner", "outer"), "heads"),
        check_vma=False,
    )
```

```python
import functools
import math

import jax
import jax.numpy as jnp
from jax import lax
from jax.experimental import pallas as pl
from jax.experimental.pallas import tpu as pltpu
from jax.sharding import PartitionSpec as P

BLOCK = 128
HEAD = 128
TILE = 4
UNIT = 4 * BLOCK
LOWEST = -1e30
AXES = ("inner", "outer")


def dot(a, b, contract):
    return lax.dot_general(a, b, (contract, ((), ())), preferred_element_type=jnp.float32)


def in_hbm(x):
    return pltpu.with_memory_space_constraint(x, pltpu.HBM)


def plan_order(chain_ref, depth_ref, order, stages):
    inner = lax.axis_index("inner")
    outer = lax.axis_index("outer")
    core = jnp.bitwise_and(inner, 1)
    q_chain, q_depth, counts = [], [], []
    for qb in range(2):
        own = (inner * 8 + outer) * 2 + qb
        q_chain.append(chain_ref[own])
        q_depth.append(depth_ref[own])
        counts.append(jnp.int32(0))
    row = 0
    for j, pieces in enumerate(stages):
        for flip, even, odd in pieces:
            offset = even + core * (odd - even)
            source = (jnp.bitwise_xor(inner, flip) * 8 + lax.rem(outer + offset + 8, 8)) * 2
            for b in range(2):
                chain = chain_ref[source + b]
                depth = depth_ref[source + b]
                for qb in range(2):
                    seen = ((chain == 0) | (chain == q_chain[qb])) & (depth < q_depth[qb])
                    order[qb, counts[qb]] = row + b * BLOCK
                    counts[qb] = counts[qb] + seen.astype(jnp.int32)
            row += UNIT
        for qb in range(2):
            order[qb, 64 + j] = counts[qb]


def attend_kernel(*refs, stage, stages, start, count_in, heads):
    first, final = stage == 0, stage == len(stages) - 1
    flushed = (len(stages) - 2, len(stages) - 1)
    refs = list(refs)
    if first:
        chain_hbm, depth_hbm, q_hbm = refs[:3]
        piece_refs = refs[3: 3 + count_in]
        kv_buf, shift, acc, q_ref, order, chain_ref, depth_ref, sem, table_sem, q_sem = refs[3 + count_in:]
    else:
        order = refs[0]
        piece_refs = refs[1: 1 + count_in]
        q_ref = refs[1 + count_in]
        refs = refs[5 + count_in:]
        if final:
            o_ref = refs.pop(0)
            out_buf, out_sem = refs[4:]
        kv_buf, shift, acc, sem = refs[:4]
    copies = []
    for ref in piece_refs:
        rows = ref.shape[0]
        copies.append(pltpu.make_async_copy(ref, kv_buf.at[pl.ds(start, rows), :], sem))
        start += rows
    if first:
        tables = [
            pltpu.make_async_copy(chain_hbm, chain_ref, table_sem.at[0]),
            pltpu.make_async_copy(depth_hbm, depth_ref, table_sem.at[1]),
        ]
        copies.append(pltpu.make_async_copy(q_hbm, q_ref, q_sem))
        for copy in tables + copies:
            copy.start()
        for copy in tables:
            copy.wait()
        plan_order(chain_ref, depth_ref, order, stages)
    else:
        for copy in copies:
            copy.start()
    for copy in copies:
        copy.wait()
    scale = HEAD ** -0.5 * math.log2(math.e)
    width = heads * BLOCK

    def heads_of(qb):
        rows = pl.ds(pl.multiple_of(qb * BLOCK, BLOCK), BLOCK)
        return jnp.concatenate([q_ref[rows, h * HEAD:(h + 1) * HEAD] for h in range(heads)], axis=0)

    def keys_of(row):
        return kv_buf[pl.ds(pl.multiple_of(row, BLOCK), BLOCK), :]

    def values_of(row):
        return kv_buf[pl.ds(pl.multiple_of(row + 2 * BLOCK, BLOCK), BLOCK), :]

    def with_ones(v):
        return jnp.concatenate([v, jnp.ones((16, v.shape[1]), v.dtype)], axis=0)

    def diagonal(qb):
        row = qb * BLOCK
        s = dot(keys_of(row), heads_of(qb), ((1,), (1,)))
        key = lax.broadcasted_iota(jnp.int32, s.shape, 0)
        query = lax.broadcasted_iota(jnp.int32, s.shape, 1)
        s = jnp.where(key <= lax.rem(query, BLOCK), s, LOWEST)
        top = jnp.max(s, axis=0, keepdims=True)
        weights = jnp.exp2((s - top) * scale).astype(jnp.bfloat16)
        shift[qb] = top
        acc[qb] = dot(with_ones(values_of(row)), weights, ((1,), (0,)))

    def tile_of(qb, at, left, size):
        rows = [order[qb, at]]
        rows += [jnp.where(i < left, order[qb, at + i], rows[0]) for i in range(1, size)]
        k = jnp.concatenate([keys_of(r) for r in rows], axis=0)
        v = with_ones(jnp.concatenate([values_of(r) for r in rows], axis=1))
        col = lax.broadcasted_iota(jnp.int32, v.shape, 1)
        v = jnp.where(col < left * BLOCK, v, jnp.zeros_like(v))
        return k, v

    def fast_tile(qb, at, left, size=TILE):
        k, v = tile_of(qb, at, left, size)
        s = dot(k, heads_of(qb), ((1,), (1,)))
        weights = jnp.exp2((s - shift[qb]) * scale).astype(jnp.bfloat16)
        acc[qb] += dot(v, weights, ((1,), (0,)))

    def safe_tile(qb, at, left):
        k, v = tile_of(qb, at, left, TILE)
        s = dot(k, heads_of(qb), ((1,), (1,)))
        before = shift[qb]
        after = jnp.maximum(before, jnp.max(s, axis=0, keepdims=True))
        weights = jnp.exp2((s - after) * scale).astype(jnp.bfloat16)
        shift[qb] = after
        acc[qb] = acc[qb] * jnp.exp2((before - after) * scale) + dot(v, weights, ((1,), (0,)))

    def out_copy(qb):
        rows = pl.ds(pl.multiple_of(qb * BLOCK, BLOCK), BLOCK)
        return pltpu.make_async_copy(out_buf.at[rows, :], o_ref.at[rows, :], out_sem.at[qb])

    def one_block(qb, _):
        now = order[qb, 64 + stage]
        if first:
            diagonal(qb)
            done = 0
        else:
            done = order[qb, 64 + stage - 1]
            if stage - 1 not in flushed:
                done = lax.div(done, TILE) * TILE
        full = lax.div(now - done, TILE)
        wide = lax.div(full, 2)

        def step(t, _):
            fast_tile(qb, done + t * 2 * TILE, 2 * TILE, 2 * TILE)
            return 0

        if len(stages[stage]) > 2:
            lax.fori_loop(0, wide, step, 0)

            @pl.when(full > 2 * wide)
            def _():
                fast_tile(qb, done + wide * 2 * TILE, TILE)

        elif not first:

            @pl.when(full > 0)
            def _():
                fast_tile(qb, done, TILE)

        if stage in flushed:
            at = done + full * TILE
            for size, wanted in ((2, now - at <= 2), (TILE, now - at > 2)):

                @pl.when((now > at) & wanted)
                def _():
                    fast_tile(qb, at, now - at, size)

        if final:
            total = acc[qb, HEAD:HEAD + 1, :]
            fine = jnp.min(jnp.where(total < 2.0 ** 64, 1.0, 0.0))

            @pl.when(fine < 0.5)
            def _():
                diagonal(qb)

                def again(t, _):
                    safe_tile(qb, t * TILE, now - t * TILE)
                    return 0

                lax.fori_loop(0, lax.div(now + TILE - 1, TILE), again, 0)

            inverse = 1.0 / acc[qb, HEAD:HEAD + 1, :]
            mixed = (acc[qb, :HEAD, :] * inverse).astype(jnp.bfloat16)
            rows = pl.ds(pl.multiple_of(qb * BLOCK, BLOCK), BLOCK)
            for h in range(heads):
                part = mixed[:, h * BLOCK:(h + 1) * BLOCK]
                out_buf[rows, h * HEAD:(h + 1) * HEAD] = part.T
            out_copy(qb).start()
        return 0

    lax.fori_loop(0, 2, one_block, 0)
    if final:
        for qb in range(2):
            out_copy(qb).wait()


def attend(queries, chain, depth, stages, stage, arrays, state):
    rows, width = queries.shape
    heads = width // HEAD
    first, final = stage == 0, stage == len(stages) - 1
    vmem = pl.BlockSpec(memory_space=pltpu.VMEM)
    smem = pl.BlockSpec(memory_space=pltpu.SMEM)
    anywhere = pl.BlockSpec(memory_space=pl.ANY)
    hbm = pl.BlockSpec(memory_space=pltpu.HBM)
    units = sum(len(p) for p in stages)
    start = UNIT * sum(len(p) for p in stages[:stage])
    held = [
        pltpu.VMEM((units * UNIT, HEAD), jnp.bfloat16),
        pltpu.VMEM((2, 1, heads * BLOCK), jnp.float32),
        pltpu.VMEM((2, HEAD + 16, heads * BLOCK), jnp.float32),
    ]
    out = jax.ShapeDtypeStruct((rows, width), jnp.bfloat16)
    n = len(arrays)
    body = functools.partial(
        attend_kernel, stage=stage, stages=stages, start=start, count_in=n, heads=heads
    )
    params = pltpu.CompilerParams(vmem_limit_bytes=32 << 20)
    sem = pltpu.SemaphoreType.DMA(())
    pairs = len(stages[stage]) * 2
    cost = pl.CostEstimate(
        flops=pairs * 4 * heads * BLOCK * BLOCK * HEAD,
        transcendentals=pairs * heads * BLOCK * BLOCK,
        bytes_accessed=pairs * BLOCK * HEAD * 4 + rows * width * 2,
    )
    if first:
        blocks = chain.shape[0]
        return pl.pallas_call(
            body,
            out_shape=held
            + [pltpu.VMEM((rows, width), jnp.bfloat16), jax.ShapeDtypeStruct((2, 128), jnp.int32)],
            in_specs=[hbm] * 3 + [anywhere] * n,
            out_specs=[vmem] * 4 + [smem],
            scratch_shapes=[
                pltpu.SMEM((blocks,), jnp.int32),
                pltpu.SMEM((blocks,), jnp.int32),
                sem,
                pltpu.SemaphoreType.DMA((2,)),
                sem,
            ],
            compiler_params=params,
            cost_estimate=cost,
            name="attend_first",
        )(*(in_hbm(x) for x in (chain, depth, queries)), *arrays)
    kv_buf, shift, acc, q_held, order = state
    result = pl.pallas_call(
        body,
        out_shape=([out] if final else []) + held,
        in_specs=[smem] + [anywhere] * n + [vmem] * 4,
        out_specs=([hbm] if final else []) + [vmem] * 3,
        input_output_aliases={2 + n + i: i + final for i in range(3)},
        scratch_shapes=[sem]
        + ([pltpu.VMEM(out.shape, out.dtype), pltpu.SemaphoreType.DMA((2,))] if final else []),
        compiler_params=params,
        cost_estimate=cost,
        name="attend_last" if final else "attend_next",
    )(order, *arrays, q_held, kv_buf, shift, acc)
    return result[0] if final else (*result, q_held, order)


def pack_kernel(k_ref, v_ref, o_ref):
    for b in range(2):
        rows = slice(b * BLOCK, (b + 1) * BLOCK)
        o_ref[b * BLOCK:(b + 1) * BLOCK, :] = k_ref[rows, :]
        o_ref[(2 + b) * BLOCK:(3 + b) * BLOCK, :] = v_ref[rows, :].T


def pack(keys, values):
    vmem = pl.BlockSpec(memory_space=pltpu.VMEM)
    return pl.pallas_call(
        pack_kernel,
        out_shape=pltpu.VMEM((UNIT, HEAD), keys.dtype),
        in_specs=[vmem, vmem],
        out_specs=vmem,
        name="pack",
    )(keys, values)


def send(x, route):
    pairs = []
    for i in range(4):
        for o in range(8):
            j, p = route(i, o)
            pairs.append((i * 8 + o, j * 8 + p % 8))
    return lax.ppermute(x, AXES, pairs)


def to_core(x):
    return send(x, lambda i, o: (i ^ 1, o))


def to_x(x):
    return send(x, lambda i, o: (i ^ 2, o))


def ring(x):
    return send(x, lambda i, o: (i, o - 1 if i % 2 else o + 1))


def local(queries, keys, values, block_chain, block_depth):
    unit = pack(keys, values)
    own = [[(f, -d, d) for f in (0, 1)] for d in range(5)]
    own_x = [[(f ^ 2, -d, d) for f in (0, 1)] for d in range(5)]
    other = [[(f ^ 1, d, -d) for f in (0, 1)] for d in range(5)]
    other_x = [[(f ^ 3, d, -d) for f in (0, 1)] for d in range(5)]
    stages = [
        own[0],
        own_x[0] + own[1] + other[1],
        own[2] + own_x[1] + other[2],
        own[3] + own_x[2] + other[3] + other_x[1],
        own[4] + own_x[3] + other_x[2],
        other_x[3] + own_x[4],
    ]
    run = functools.partial(attend, queries, block_chain, block_depth, stages)

    def meet(*xs):
        return lax.optimization_barrier(xs)

    r0 = jnp.concatenate([unit, to_core(unit)], axis=0)
    x0, r1 = to_x(r0), ring(r0)
    state = run(0, [r0], None)
    r1, state = meet(r1, state)
    x1, c1, r2 = to_x(r1), to_core(r1), ring(r1)
    state = run(1, [x0, r1, c1], state)
    r2, state = meet(r2, state)
    x2, c2, r3, cx1 = to_x(r2), to_core(r2), ring(r2), to_core(x1)
    state = run(2, [r2, x1, c2], state)
    r3, state = meet(r3, state)
    x3, c3, r4, cx2 = to_x(r3), to_core(r3), ring(r3), to_core(x2)
    state = run(3, [r3, x2, c3, cx1], state)
    r4, x3, state = meet(r4, x3, state)
    x4, cx3 = to_x(r4), to_core(x3)
    state = run(4, [r4, x3, cx2], state)
    return run(5, [cx3, x4], state)


def solution(mesh):
    return jax.shard_map(
        local,
        mesh=mesh,
        in_specs=(
            P(("inner", "outer"), "heads"),
            P(("inner", "outer"), "heads"),
            P(("inner", "outer"), "heads"),
            P(),
            P(),
        ),
        out_specs=P(("inner", "outer"), "heads"),
        check_vma=False,
    )
```
